512 devices in a mesh: dp: 32 (over z_hi, y), space: 16 (over x, z_lo, core).
Axes of the slice: x: 4, y: 8, z: 8 (z_hi: 4, z_lo: 2; z = z_hi * 2 + z_lo), core: 2. Of those that a mesh axis runs over, the one named last changes fastest.
Arguments:
- activations: bfloat16 [32, 64, 32, 48, 128], P('dp', None, 'space'), may hold values from -6 to 6
- cotangent: bfloat16 [32, 64, 32, 48, 128], P('dp', None, 'space'), may hold values from -6 to 6
- mode_weights: bfloat16 [2048, 64, 128], P(('space', 'dp')), may hold values from -6 to 6
- pointwise: bfloat16 [64, 64], replicated, may hold values from -0.75 to 0.75
- offsets: float32 [64], replicated, may hold values from -3 to 3
Outputs:
- grad_in: bfloat16 [32, 64, 32, 48, 128], P('dp', None, 'space')
- grad_spectral: float32 [2048, 64, 128], P(('space', 'dp'))
The draws below stay inside these ranges and needn't reach their ends.
All inputs are finite; a program needn't handle non-finite values.
Results may differ from the reference program's by a relative error of at most 0.02.
Values may be sent and summed in bfloat16 or wider, within the bound.
A program may use at most 64 MiB of HBM per device.

```python
import math
import jax
import jax.numpy as jnp
from jax import lax

C = 64
MX = 16
MY = 16
MZ = 8
NX = 32
NY = 48
NZ = 128
BATCH = 32
MODES = 2048


def block_scale(stream_key, shape, shards, low, high):
    def one(position, parts):
        steps = jax.random.uniform(jax.random.fold_in(jax.random.fold_in(stream_key, 6), position), (parts,), jnp.float32, low / len(shards), high / len(shards))
        return jnp.repeat(jnp.exp(steps), shape[position] // parts).reshape((-1,) + (1,) * (len(shape) - position - 1))

    loudness = one(*shards[0])
    for cut in shards[1:]:
        loudness = loudness * one(*cut)
    return loudness


def gaussian(rng, dims, width, bound, pieces=(), kind=jnp.bfloat16):
    drawn = width * jax.random.normal(rng, dims, jnp.float32)
    if pieces:
        drawn = drawn * block_scale(rng, dims, pieces, -0.22, 0.18)
    return jnp.clip(drawn, -bound, bound).astype(kind)


def setup_inputs(seed: int = 0) -> dict:
    keys = jax.random.split(jax.random.key(seed), 6)
    activations = gaussian(keys[0], (BATCH, C, NX, NY, NZ), 1.0, 6.0, ((0, 32), (2, 16)))
    cotangent = gaussian(keys[1], (BATCH, C, NX, NY, NZ), 1.0, 6.0, ((0, 32), (2, 16)))
    mode_weights = gaussian(keys[2], (MODES, C, 2 * C), 1.0, 6.0, ((0, 512),))
    pointwise = gaussian(keys[3], (C, C), C ** -0.5, 0.75)
    offsets = gaussian(keys[4], (C,), 0.5, 3.0, (), jnp.float32)
    return dict(activations=activations, cotangent=cotangent, mode_weights=mode_weights, pointwise=pointwise, offsets=offsets)


def centered(count):
    index = jnp.arange(count, dtype=jnp.int32)
    return jnp.where(index < count // 2, index, index - count)


def plane_tables(rows_y, rows_z, modes_y, modes_z):
    along_y = jnp.arange(rows_y, dtype=jnp.int32)[:, None, None, None]
    along_z = jnp.arange(rows_z, dtype=jnp.int32)[None, :, None, None]
    freq_y = centered(modes_y)[None, None, :, None]
    freq_z = jnp.arange(modes_z, dtype=jnp.int32)[None, None, None, :]
    phase = jnp.mod(freq_y * along_y * rows_z + freq_z * along_z * rows_y, rows_y * rows_z)
    theta = phase.astype(jnp.float32) * (2.0 * math.pi / (rows_y * rows_z))
    cosine = jnp.cos(theta)
    sine = jnp.sin(theta)
    forward = jnp.stack([cosine, -sine], -1).reshape(rows_y * rows_z, modes_y * modes_z * 2)
    scaled = jnp.where(freq_z == 0, 1.0, 2.0).astype(jnp.float32) / (rows_y * rows_z)
    inverse = jnp.stack([cosine * scaled, -sine * scaled], -1).reshape(rows_y * rows_z, modes_y * modes_z * 2).T
    return forward.astype(jnp.bfloat16), inverse.astype(jnp.bfloat16)


def line_tables(length, modes):
    along = jnp.arange(length, dtype=jnp.int32)[:, None]
    freq = centered(modes)[None, :]
    phase = jnp.mod(freq * along, length)
    theta = phase.astype(jnp.float32) * (2.0 * math.pi / length)
    cosine = jnp.cos(theta)
    sine = jnp.sin(theta)
    first = jnp.stack([cosine, -sine], -1)
    second = jnp.stack([sine, cosine], -1)
    forward = jnp.stack([first, second], 1).reshape(2 * length, 2 * modes)
    inv_first = jnp.stack([cosine.T, sine.T], -1) / length
    inv_second = jnp.stack([-sine.T, cosine.T], -1) / length
    inverse = jnp.stack([inv_first, inv_second], 1).reshape(2 * modes, 2 * length)
    return forward.astype(jnp.bfloat16), inverse.astype(jnp.bfloat16)


def expand_weights(weights):
    half = weights.shape[1]
    real_part = weights[:, :, :half]
    imag_part = weights[:, :, half:]
    upper = jnp.concatenate([real_part, imag_part], axis=2)
    lower = jnp.concatenate([-imag_part, real_part], axis=2)
    return jnp.concatenate([upper, lower], axis=1)


def outer_sum(left, right):
    return jnp.einsum("mbi,mbo->mio", left.astype(jnp.float32), right.astype(jnp.float32), precision=lax.Precision.HIGHEST)


def weight_terms(spec_in, spec_grad):
    half = spec_in.shape[2] // 2
    in_real = spec_in[:, :, :half]
    in_imag = spec_in[:, :, half:]
    gr_real = spec_grad[:, :, :half]
    gr_imag = spec_grad[:, :, half:]
    real_term = outer_sum(in_real, gr_real) + outer_sum(in_imag, gr_imag)
    imag_term = outer_sum(in_real, gr_imag) - outer_sum(in_imag, gr_real)
    return jnp.concatenate([real_term, imag_term], axis=2)


def product(left, right, form):
    return jnp.einsum(form, left.astype(jnp.float32), right.astype(jnp.float32), precision=lax.Precision.HIGHEST)


def to_spectra(planes, table):
    planes_yz = MY * MZ
    lines = planes.reshape(C, NX, planes_yz, 2).transpose(0, 2, 1, 3).reshape(C, planes_yz, 2 * NX)
    spectra = product(lines, table, "cpl,lk->cpk").astype(jnp.bfloat16)
    return spectra.reshape(C, planes_yz, MX, 2).transpose(1, 2, 3, 0).reshape(MODES, 2 * C)


def to_planes(spectra, table):
    planes_yz = MY * MZ
    lines = spectra.reshape(planes_yz, MX, 2, C).transpose(3, 0, 1, 2).reshape(C, planes_yz, 2 * MX)
    lines = product(lines, table, "cpk,kl->cpl").astype(jnp.bfloat16)
    return lines.reshape(C, planes_yz, NX, 2).transpose(0, 2, 1, 3).reshape(C, NX, 2 * planes_yz)


def gelu_slope(value):
    cdf = 0.5 * (1.0 + lax.erf(value * 0.7071067811865476))
    density = jnp.exp(-0.5 * value * value) * 0.3989422804014327
    return cdf + value * density


def reference(activations, cotangent, mode_weights, pointwise, offsets):
    plane_fwd, plane_inv = plane_tables(NY, NZ, MY, MZ)
    line_fwd, line_inv = line_tables(NX, MX)
    blocks = expand_weights(mode_weights)

    def one_sample(pair):
        field, upstream = pair
        flat = field.reshape(C, NX, NY * NZ)
        planes = product(flat, plane_fwd, "cxn,nk->cxk").astype(jnp.bfloat16)
        spec_in = to_spectra(planes, line_fwd)
        spec_out = product(spec_in, blocks, "mi,mio->mo").astype(jnp.bfloat16)
        line_back = to_planes(spec_out, line_inv)
        spectral = product(line_back, plane_inv, "cxk,kn->cxn")
        local_part = product(pointwise, flat, "io,ixn->oxn")
        summed = spectral + local_part + offsets[:, None, None]
        slope_grad = (upstream.reshape(C, NX, NY * NZ).astype(jnp.float32) * gelu_slope(summed)).astype(jnp.bfloat16)
        back_plane = product(slope_grad, plane_inv, "cxn,kn->cxk").astype(jnp.bfloat16)
        spec_grad = to_spectra(back_plane, line_inv.T)
        spec_dx = product(spec_grad, blocks, "mo,mio->mi").astype(jnp.bfloat16)
        line_dx = to_planes(spec_dx, line_fwd.T)
        total = product(line_dx, plane_fwd, "cxk,nk->cxn") + product(pointwise, slope_grad, "io,oxn->ixn")
        return total.astype(jnp.bfloat16).reshape(C, NX, NY, NZ), spec_in, spec_grad

    grad_in, all_in, all_grad = lax.map(one_sample, (activations, cotangent))
    grad_spectral = weight_terms(all_in.transpose(1, 0, 2), all_grad.transpose(1, 0, 2))
    return grad_in, grad_spectral
```

```python
import jax
import jax.numpy as jnp
import numpy as np
from jax import lax
from jax.experimental import pallas as pl
from jax.experimental.pallas import tpu as pltpu
from jax.sharding import PartitionSpec as P

MX, MY, MZ = 16, 16, 8
NX, NY, NZ = 32, 48, 128
C = 64
GRP = 8
MESH = pl.DeviceIdType.MESH
F32, BF16 = jnp.float32, jnp.bfloat16


def centered(count):
    index = np.arange(count)
    return np.where(index < count // 2, index, index - count)


def tables():
    ty = 2 * np.pi * centered(MY)[:, None] * np.arange(NY)[None, :] / NY
    along_y = np.stack([np.cos(ty), -np.sin(ty)], 1)
    eye = np.eye(GRP)
    to_y = np.einsum("jry,cd->jrcdy", along_y, eye).reshape(MY * 2 * GRP, GRP * NY)
    tz = 2 * np.pi * np.arange(MZ)[:, None] * np.arange(NZ)[None, :] / NZ
    along_z = np.zeros((MZ, 2, 2, NZ))
    along_z[:, 0, 0], along_z[:, 0, 1] = np.cos(tz), np.sin(tz)
    along_z[:, 1, 0], along_z[:, 1, 1] = -np.sin(tz), np.cos(tz)
    weight = np.where(np.arange(MZ) == 0, 1.0, 2.0)[:, None, None, None]
    plain = along_z.reshape(MZ * 2, 2 * NZ)
    weighted = (along_z * weight).reshape(MZ * 2, 2 * NZ)
    s = 2 * np.pi * centered(MX)[None, :] * np.arange(NX)[:, None] / NX
    line = np.zeros((NX, 2, MX, 2))
    line[:, 0, :, 0], line[:, 0, :, 1] = np.cos(s), -np.sin(s)
    line[:, 1, :, 0], line[:, 1, :, 1] = np.sin(s), np.cos(s)
    line = line.reshape(NX // 2, 2, 2, MX, 2)
    to_q = np.einsum("shuqa,bd,ke->hakqbdseu", line, np.eye(4), np.eye(2)).reshape(512, 256)
    to_x = np.einsum("shuqa,bd,ke->habskueqd", line, np.eye(4), np.eye(2)).reshape(1024, 128)
    cast = lambda t: np.asarray(t.astype(np.float32)).astype(jnp.bfloat16)
    return tuple(cast(t) for t in (to_y, to_y.T.copy(), plain, weighted, to_q, to_x))


def dot(a, b, dims=((1,), (0,))):
    return lax.dot_general(a, b, (dims, ((), ())), preferred_element_type=F32)


def gelu_slope(value):
    cdf = 0.5 * (1.0 + lax.erf(value * 0.7071067811865476))
    density = jnp.exp(-0.5 * value * value) * 0.3989422804014327
    return cdf + value * density


def kernel(
    act_h, cot_h, w_h, pw_ref, off_ref, by_h, byt_h, fz_h, fzw_h, bq_h, bx_h,
    out_h, gs_h,
    act, cot, w_own, by, byt, fz, fzw, bq, bx,
    mid, loc, slope, outb, offb, kron, wall, wbuf, spec, xin, din, gsb,
    send, back, land,
    in_sem, tab_sem, w_sem, out_sem, ssem, rsem, wssem, wrsem, xssem, xrsem,
):
    dp = lax.axis_index("dp")
    s = lax.axis_index("space")
    zh, y = dp // 8, dp % 8
    me = zh * 16 + s
    low = lax.broadcasted_iota(jnp.int32, (1, 128), 1) < 64

    def at(tt):
        return ((tt // 16) * 8 + y, tt % 16)

    bar = pltpu.get_barrier_semaphore()

    def hello(t, c):
        pl.semaphore_signal(bar, inc=1, device_id=at((me + t) % 64), device_id_type=MESH)
        return c

    def hello_y(t, c):
        pl.semaphore_signal(bar, inc=1, device_id=(zh * 8 + (y + t) % 8, s), device_id_type=MESH)
        return c

    def act_copy(g):
        rows = pl.ds(g * GRP, GRP)
        return pltpu.make_async_copy(act_h.at[rows], act.at[rows], in_sem.at[g])

    tabs = [
        pltpu.make_async_copy(h, v, tab_sem.at[i])
        for i, (h, v) in enumerate(
            ((by_h, by), (fz_h, fz), (bq_h, bq), (bx_h, bx), (byt_h, byt), (fzw_h, fzw), (cot_h, cot))
        )
    ]
    own_w = pltpu.make_async_copy(w_h, w_own, w_sem)
    tabs[0].start()
    for g in range(8):
        act_copy(g).start()
    own_w.start()
    for t in tabs[1:]:
        t.start()
    lax.fori_loop(1, 64, hello, 0)
    lax.fori_loop(1, 8, hello_y, 0)

    def lanes(ref, g):
        rows = pl.ds(g * GRP, GRP)
        return jnp.concatenate(
            [ref[rows, x].reshape(GRP * NY, NZ) for x in range(2)], axis=1
        )

    def put_mid(g, res):
        for x in range(2):
            rows = pl.ds(pl.multiple_of(x * 64 + g * GRP, GRP), GRP)
            mid[:, rows, :] = res[:, x * NZ:(x + 1) * NZ].reshape(2 * MY, GRP, NZ)

    def get_mid(g):
        parts = []
        for x in range(2):
            rows = pl.ds(pl.multiple_of(x * 64 + g * GRP, GRP), GRP)
            parts.append(mid[:, rows, :].reshape(2 * MY * GRP, NZ).astype(BF16))
        return jnp.concatenate(parts, axis=1)

    def z_and_send(table, sbuf, st):
        for bt in range(4):
            for u in range(4):
                j = (s + 1 + bt * 4 + u) % 16
                pair = jnp.concatenate([mid[2 * j].astype(BF16), mid[2 * j + 1].astype(BF16)], axis=1)
                res = dot(table[...], pair, ((1,), (1,)))
                sbuf[pl.ds(j * 4, 4)] = res.astype(BF16).reshape(4, 4, 128)

            def one(n, c):
                j = (s + 1 + bt * 4 + n // 4) % 16
                z = (zh + 1 + n % 4) % 4
                pltpu.make_async_remote_copy(
                    sbuf.at[j * 4 + z], land.at[st, me], ssem.at[st], rsem.at[st],
                    device_id=(z * 8 + y, j), device_id_type=MESH,
                ).start()
                return c

            lax.fori_loop(0, 16 if bt < 3 else 15, one, 0)
        pltpu.make_async_copy(sbuf.at[s * 4 + zh], land.at[st, me], rsem.at[st]).start()

    def send_back(sbuf, st):
        def one(t, c):
            tt = (me + t) % 64
            pltpu.make_async_remote_copy(
                sbuf.at[tt], land.at[st, s * 4 + zh], ssem.at[st], rsem.at[st],
                device_id=at(tt), device_id_type=MESH,
            ).start()
            return c

        lax.fori_loop(1, 64, one, 0)
        pltpu.make_async_copy(sbuf.at[me], land.at[st, s * 4 + zh], rsem.at[st]).start()

    def landed(st):
        whole = land.at[st]
        pltpu.make_async_copy(whole, whole, rsem.at[st]).wait()

    def share(src, dst, k):
        def one(t, c):
            yy = (y + t) % 8
            pltpu.make_async_remote_copy(
                src.at[yy], dst.at[y], xssem.at[k], xrsem.at[k],
                device_id=(zh * 8 + yy, s), device_id_type=MESH,
            ).start()
            return c

        lax.fori_loop(1, 8, one, 0)
        pltpu.make_async_copy(src.at[y], dst.at[y], xrsem.at[k]).start()

    def to_modes(st, scale):
        r = dot(bq[...], land[st].reshape(256, 128))
        first = jnp.where(low, r[0:128], r[384:512])
        second = jnp.where(low, r[128:256], r[256:384])
        return ((first + pltpu.roll(second, 64, 1)) * scale).astype(BF16)

    def from_modes(mixed, scale):
        r = dot(bx[...], mixed)
        first = jnp.where(low, r[0:256], r[768:1024])
        second = jnp.where(low, r[512:768], r[256:512])
        return ((first + pltpu.roll(second, 64, 1)) * scale).astype(BF16)

    def inverse_z(st, table):
        rows = land[st].reshape(256, 128)
        for j in range(16):
            res = dot(rows[16 * j:16 * (j + 1)], table[...], ((0,), (0,)))
            mid[2 * j] = res[:, :NZ]
            mid[2 * j + 1] = res[:, NZ:]

    which = (lax.broadcasted_iota(jnp.int32, (16, 1), 0) // 4)

    def kron_of(dims):
        rep = (
            lax.broadcasted_iota(jnp.int32, (1024, 64), 0) // 16
            == lax.broadcasted_iota(jnp.int32, (1024, 64), 1)
        ).astype(F32).astype(BF16)
        half = dot(rep, pw_ref[...], dims).astype(BF16)
        for m in range(4):
            full = dot(half[256 * m:256 * (m + 1)], rep, ((1,), (1,)))
            same = (
                lax.broadcasted_iota(jnp.int32, (256, 1024), 0) % 16
                == lax.broadcasted_iota(jnp.int32, (256, 1024), 1) % 16
            )
            kron[256 * m:256 * (m + 1), :] = jnp.where(same, full, 0.0).astype(BF16)

    def pointwise(src, with_offset):
        def step(n, c):
            yb, m = n // 4, n % 4
            rows = pl.ds(pl.multiple_of(yb * 16, 16), 16)
            rhs = jnp.concatenate([src[:, x, rows, :].reshape(1024, NZ) for x in range(2)], axis=1)
            res = dot(kron[pl.ds(pl.multiple_of(m * 256, 256), 256), :], rhs)
            for x in range(2):
                part = res[:, x * NZ:(x + 1) * NZ].reshape(16, 2, 8, NZ)
                if with_offset:
                    part = part + offb[pl.ds(m * 16, 16)][:, None]
                loc[pl.ds(m * 16, 16), x, rows, :] = part.reshape(16, 16, NZ)
            return c

        lax.fori_loop(0, 12, step, 0)

    tabs[0].wait()

    def forward(g, c):
        act_copy(g).wait()
        put_mid(g, dot(by[...], lanes(act, g)))
        return c

    lax.fori_loop(0, 8, forward, 0)
    own_w.wait()
    tabs[1].wait()
    pl.semaphore_wait(bar, 70)

    def send_w(t, c):
        pltpu.make_async_remote_copy(
            w_own, wbuf.at[y], wssem, wrsem, device_id=(zh * 8 + (y + t) % 8, s), device_id_type=MESH
        ).start()
        return c

    z_and_send(fz, send.at[0], 0)
    lax.fori_loop(1, 8, send_w, 0)
    pltpu.make_async_copy(w_own, wbuf.at[y], wrsem).start()

    for t in tabs[2:]:
        t.wait()

    def spread(o, c):
        offb[o] = jnp.full((8, NZ), off_ref[o], F32)
        return c

    lax.fori_loop(0, C, spread, 0)
    kron_of(((1,), (1,)))

    pltpu.make_async_copy(wbuf, wbuf, wrsem).wait()

    def widen(n, c):
        w = wbuf[n // 4, n % 4]
        wf = w.astype(F32)
        turned = pltpu.roll(wf, 64, 1)
        wall[n, 0:64, :] = w
        wall[n, 64:128, :] = jnp.where(low, -turned, turned).astype(BF16)
        return c

    lax.fori_loop(0, 32, widen, 0)

    landed(0)
    spec_in = to_modes(0, 1.0)
    spec[0] = spec_in.reshape(8, 16, 128)
    share(spec.at[0], xin, 0)
    mixed = []
    for t in range(8):
        x = spec_in[16 * t:16 * (t + 1)].astype(F32)
        x4 = jnp.concatenate([jnp.where(which == i, x, 0.0) for i in range(4)], axis=1).astype(BF16)
        mixed.append(dot(x4, wall[4 * t:4 * (t + 1)].reshape(512, 128)))
    mixed = jnp.concatenate(mixed, axis=0).astype(BF16)
    back[0] = from_modes(mixed, 1.0 / (NX * NY * NZ)).reshape(64, 4, 128)
    send_back(back.at[0], 1)
    pointwise(act, True)

    landed(1)
    inverse_z(1, fzw)

    def middle(g, c):
        rows = pl.ds(g * GRP, GRP)
        field = dot(byt[...], get_mid(g))
        halves = []
        for x in range(2):
            value = field[:, x * NZ:(x + 1) * NZ].reshape(GRP, NY, NZ) + loc[rows, x]
            grad = (cot[rows, x].astype(F32) * gelu_slope(value)).astype(BF16)
            slope[rows, x] = grad
            halves.append(grad.reshape(GRP * NY, NZ))
        put_mid(g, dot(by[...], jnp.concatenate(halves, axis=1)))
        return c

    lax.fori_loop(0, 8, middle, 0)
    z_and_send(fzw, send.at[1], 2)
    kron_of(((1,), (0,)))

    landed(2)
    spec_grad = to_modes(2, 1.0 / (NX * NY * NZ))
    spec[1] = spec_grad.reshape(8, 16, 128)
    share(spec.at[1], din, 1)
    mixed = []
    for t in range(8):
        res = dot(spec_grad[16 * t:16 * (t + 1)], wall[4 * t:4 * (t + 1)].reshape(512, 128), ((1,), (1,)))
        total = jnp.where(which == 0, res[:, 0:128], 0.0)
        for i in range(1, 4):
            total = total + jnp.where(which == i, res[:, 128 * i:128 * (i + 1)], 0.0)
        mixed.append(total)
    mixed = jnp.concatenate(mixed, axis=0).astype(BF16)
    back[1] = from_modes(mixed, 1.0).reshape(64, 4, 128)
    send_back(back.at[1], 3)
    pointwise(slope, False)

    for k, buf in enumerate((xin, din)):
        pltpu.make_async_copy(buf, buf, xrsem.at[k]).wait()
    left = xin[...].reshape(128, 128).astype(F32)
    right = din[...].reshape(128, 128)
    mode = lax.broadcasted_iota(jnp.int32, (128, 1), 0) // 4 % 4
    for i in range(4):
        g = dot(jnp.where(mode == i, left, 0.0).astype(BF16), right, ((0,), (0,)))
        turned = pltpu.roll(g[64:128], 64, 1)
        gsb[i] = g[0:64] + jnp.where(low, turned, -turned)
    gs_out = pltpu.make_async_copy(gsb, gs_h, w_sem)
    gs_out.start()

    landed(3)
    inverse_z(3, fz)

    def last(g, c):
        rows = pl.ds(g * GRP, GRP)
        field = dot(byt[...], get_mid(g))
        for x in range(2):
            value = field[:, x * NZ:(x + 1) * NZ].reshape(GRP, NY, NZ) + loc[rows, x]
            outb[rows, x] = value.astype(BF16)
        pltpu.make_async_copy(outb.at[rows], out_h.at[rows], out_sem.at[g]).start()
        return c

    lax.fori_loop(0, 8, last, 0)
    for g in range(8):
        rows = pl.ds(g * GRP, GRP)
        pltpu.make_async_copy(outb.at[rows], out_h.at[rows], out_sem.at[g]).wait()
    gs_out.wait()
    for st in range(4):
        sent = land.at[st, pl.ds(0, 63)]
        pltpu.make_async_copy(sent, sent, ssem.at[st]).wait()
    sent = wbuf.at[pl.ds(0, 7)]
    pltpu.make_async_copy(sent, sent, wssem).wait()
    for k in range(2):
        sent = xin.at[pl.ds(0, 7)]
        pltpu.make_async_copy(sent, sent, xssem.at[k]).wait()


def body(activations, cotangent, mode_weights, pointwise, offsets):
    shape = (C, 2, NY, NZ)
    consts = [jnp.asarray(t) for t in tables()]
    hbm = pl.BlockSpec(memory_space=pl.ANY)
    grad_in, grad_spectral = pl.pallas_call(
        kernel,
        out_shape=(
            jax.ShapeDtypeStruct(shape, BF16),
            jax.ShapeDtypeStruct((4, C, 2 * C), F32),
        ),
        in_specs=[hbm, hbm, hbm, pl.BlockSpec(memory_space=pltpu.VMEM), pl.BlockSpec(memory_space=pltpu.SMEM)]
        + [hbm] * 6,
        out_specs=(hbm, hbm),
        scratch_shapes=[
            pltpu.VMEM(shape, BF16),
            pltpu.VMEM(shape, BF16),
            pltpu.VMEM((4, C, 2 * C), BF16),
        ]
        + [pltpu.VMEM(t.shape, BF16) for t in consts]
        + [
            pltpu.VMEM((2 * MY, 128, NZ), F32),
            pltpu.VMEM(shape, F32),
            pltpu.VMEM(shape, BF16),
            pltpu.VMEM(shape, BF16),
            pltpu.VMEM((C, 8, NZ), F32),
            pltpu.VMEM((1024, 1024), BF16),
            pltpu.VMEM((32, 128, 128), BF16),
            pltpu.VMEM((8, 4, C, 2 * C), BF16),
            pltpu.VMEM((2, 8, 16, 128), BF16),
            pltpu.VMEM((8, 16, 128), BF16),
            pltpu.VMEM((8, 16, 128), BF16),
            pltpu.VMEM((4, C, 2 * C), F32),
            pltpu.VMEM((2, 64, 4, 128), BF16),
            pltpu.VMEM((2, 64, 4, 128), BF16),
            pltpu.VMEM((4, 64, 4, 128), BF16),
            pltpu.SemaphoreType.DMA((8,)),
            pltpu.SemaphoreType.DMA((7,)),
            pltpu.SemaphoreType.DMA,
            pltpu.SemaphoreType.DMA((8,)),
            pltpu.SemaphoreType.DMA((4,)),
            pltpu.SemaphoreType.DMA((4,)),
            pltpu.SemaphoreType.DMA,
            pltpu.SemaphoreType.DMA,
            pltpu.SemaphoreType.DMA((2,)),
            pltpu.SemaphoreType.DMA((2,)),
        ],
        compiler_params=pltpu.CompilerParams(
            collective_id=0, has_side_effects=True, vmem_limit_bytes=48 << 20
        ),
    )(activations.reshape(shape), cotangent.reshape(shape), mode_weights, pointwise, offsets, *consts)
    return grad_in.reshape(activations.shape), grad_spectral


def solution(mesh):
    return jax.shard_map(
        body,
        mesh=mesh,
        in_specs=(
            P("dp", None, "space", None, None),
            P("dp", None, "space", None, None),
            P(("space", "dp"), None, None),
            P(),
            P(),
        ),
        out_specs=(P("dp", None, "space", None, None), P(("space", "dp"), None, None)),
        check_vma=False,
    )
```

```python
import jax
import jax.numpy as jnp
import numpy as np
from jax import lax
from jax.experimental import pallas as pl
from jax.experimental.pallas import tpu as pltpu
from jax.sharding import PartitionSpec as P

MX, MY, MZ = 16, 16, 8
NX, NY, NZ = 32, 48, 128
C = 64
GRP = 8
MESH = pl.DeviceIdType.MESH
F32, BF16 = jnp.float32, jnp.bfloat16


def centered(count):
    index = np.arange(count)
    return np.where(index < count // 2, index, index - count)


def tables():
    ty = 2 * np.pi * centered(MY)[:, None] * np.arange(NY)[None, :] / NY
    along_y = np.stack([np.cos(ty), -np.sin(ty)], 1)
    eye = np.eye(GRP)
    to_y = np.einsum("jry,cd->jrcdy", along_y, eye).reshape(MY * 2 * GRP, GRP * NY)
    tz = 2 * np.pi * np.arange(MZ)[:, None] * np.arange(NZ)[None, :] / NZ
    along_z = np.zeros((MZ, 2, 2, NZ))
    along_z[:, 0, 0], along_z[:, 0, 1] = np.cos(tz), np.sin(tz)
    along_z[:, 1, 0], along_z[:, 1, 1] = -np.sin(tz), np.cos(tz)
    weight = np.where(np.arange(MZ) == 0, 1.0, 2.0)[:, None, None, None]
    plain = along_z.reshape(MZ * 2, 2 * NZ)
    weighted = (along_z * weight).reshape(MZ * 2, 2 * NZ)
    s = 2 * np.pi * centered(MX)[None, :] * np.arange(NX)[:, None] / NX
    line = np.zeros((NX, 2, MX, 2))
    line[:, 0, :, 0], line[:, 0, :, 1] = np.cos(s), -np.sin(s)
    line[:, 1, :, 0], line[:, 1, :, 1] = np.sin(s), np.cos(s)
    line = line.reshape(NX // 2, 2, 2, MX, 2)
    to_q = np.einsum("shuqa,bd,ke->hakqbdseu", line, np.eye(4), np.eye(2)).reshape(512, 256)
    to_x = np.einsum("shuqa,bd,ke->habskueqd", line, np.eye(4), np.eye(2)).reshape(1024, 128)
    cast = lambda t: np.asarray(t.astype(np.float32)).astype(jnp.bfloat16)
    return tuple(cast(t) for t in (to_y, to_y.T.copy(), plain, weighted, to_q, to_x))


def dot(a, b, dims=((1,), (0,))):
    return lax.dot_general(a, b, (dims, ((), ())), preferred_element_type=F32)


def gelu_slope(value):
    cdf = 0.5 * (1.0 + lax.erf(value * 0.7071067811865476))
    density = jnp.exp(-0.5 * value * value) * 0.3989422804014327
    return cdf + value * density


def kernel(
    act_h, cot_h, w_h, pw_ref, off_ref, by_h, byt_h, fz_h, fzw_h, bq_h, bx_h,
    out_h, gs_h,
    act, cot, w_own, by, byt, fz, fzw, bq, bx,
    mid, mix, loc, slope, outb, offb, kron, wall, wbuf, spec, xin, din, gsb,
    send, back, land,
    in_sem, tab_sem, w_sem, out_sem, ssem, rsem, wssem, wrsem, xssem, xrsem,
):
    dp = lax.axis_index("dp")
    s = lax.axis_index("space")
    zh, y = dp // 8, dp % 8
    me = zh * 16 + s
    low = lax.broadcasted_iota(jnp.int32, (1, 128), 1) < 64

    def far_first(k, half):
        return half + (1 - 2 * (k % 2)) * ((k + 1) // 2)

    z = 2 * zh + s // 2 % 2

    def peer(n):
        zt = (z + far_first(n // 8, 4)) % 8
        xt = (s // 4 + far_first(n // 2 % 4, 2)) % 4
        return zt // 2, xt * 4 + zt % 2 * 2 + (s + 1 + n) % 2

    def peer_y(n):
        return (y + far_first(n, 4)) % 8

    bar = pltpu.get_barrier_semaphore()

    def hello(n, c):
        zt, st = peer(n)
        pl.semaphore_signal(bar, inc=1, device_id=(zt * 8 + y, st), device_id_type=MESH)
        return c

    def hello_y(n, c):
        pl.semaphore_signal(bar, inc=1, device_id=(zh * 8 + peer_y(n), s), device_id_type=MESH)
        return c

    def act_copy(g):
        rows = pl.ds(g * GRP, GRP)
        return pltpu.make_async_copy(act_h.at[rows], act.at[rows], in_sem.at[g])

    tabs = [
        pltpu.make_async_copy(h, v, tab_sem.at[i])
        for i, (h, v) in enumerate(
            ((by_h, by), (fz_h, fz), (bq_h, bq), (bx_h, bx), (byt_h, byt), (fzw_h, fzw), (cot_h, cot))
        )
    ]
    own_w = pltpu.make_async_copy(w_h, w_own, w_sem)
    tabs[0].start()
    for g in range(8):
        act_copy(g).start()
    own_w.start()
    for t in tabs[1:]:
        t.start()
    lax.fori_loop(0, 63, hello, 0)
    lax.fori_loop(0, 7, hello_y, 0)

    def lanes(ref, g):
        rows = pl.ds(g * GRP, GRP)
        return jnp.concatenate(
            [ref[rows, x].reshape(GRP * NY, NZ) for x in range(2)], axis=1
        )

    def put_mid(g, res):
        for x in range(2):
            rows = pl.ds(x * 64 + g * GRP, GRP)
            mid[:, rows, :] = res[:, x * NZ:(x + 1) * NZ].reshape(2 * MY, GRP, NZ)

    def get_mid(g):
        parts = []
        for x in range(2):
            rows = pl.ds(x * 64 + g * GRP, GRP)
            parts.append(mid[:, rows, :].reshape(2 * MY * GRP, NZ).astype(BF16))
        return jnp.concatenate(parts, axis=1)

    def z_and_send(table, sbuf, st):
        for j in range(16):
            pair = jnp.concatenate([mid[2 * j].astype(BF16), mid[2 * j + 1].astype(BF16)], axis=1)
            res = dot(table[...], pair, ((1,), (1,)))
            sbuf[4 * j:4 * (j + 1)] = res.astype(BF16).reshape(4, 4, 128)

        def one(n, c):
            zt, xt = peer(n)
            pltpu.make_async_remote_copy(
                sbuf.at[xt * 4 + zt], land.at[st, me], ssem.at[st], rsem.at[st],
                device_id=(zt * 8 + y, xt), device_id_type=MESH,
            ).start()
            return c

        lax.fori_loop(0, 63, one, 0)
        pltpu.make_async_copy(sbuf.at[s * 4 + zh], land.at[st, me], rsem.at[st]).start()

    def send_back(sbuf, st):
        def one(n, c):
            zt, xt = peer(n)
            pltpu.make_async_remote_copy(
                sbuf.at[zt * 16 + xt], land.at[st, s * 4 + zh], ssem.at[st], rsem.at[st],
                device_id=(zt * 8 + y, xt), device_id_type=MESH,
            ).start()
            return c

        lax.fori_loop(0, 63, one, 0)
        pltpu.make_async_copy(sbuf.at[me], land.at[st, s * 4 + zh], rsem.at[st]).start()

    def landed(st):
        whole = land.at[st]
        pltpu.make_async_copy(whole, whole, rsem.at[st]).wait()

    def share(src, dst, k):
        def one(n, c):
            yy = peer_y(n)
            pltpu.make_async_remote_copy(
                src.at[yy], dst.at[y], xssem.at[k], xrsem.at[k],
                device_id=(zh * 8 + yy, s), device_id_type=MESH,
            ).start()
            return c

        lax.fori_loop(0, 7, one, 0)
        pltpu.make_async_copy(src.at[y], dst.at[y], xrsem.at[k]).start()

    def to_modes(st, scale):
        r = dot(bq[...], land[st].reshape(256, 128))
        first = jnp.where(low, r[0:128], r[384:512])
        second = jnp.where(low, r[128:256], r[256:384])
        return ((first + pltpu.roll(second, 64, 1)) * scale).astype(BF16)

    def from_modes(mixed, scale):
        r = dot(bx[...], mixed)
        first = jnp.where(low, r[0:256], r[768:1024])
        second = jnp.where(low, r[512:768], r[256:512])
        return ((first + pltpu.roll(second, 64, 1)) * scale).astype(BF16)

    def inverse_z(st, table):
        rows = land[st].reshape(256, 128)
        for j in range(16):
            res = dot(rows[16 * j:16 * (j + 1)], table[...], ((0,), (0,)))
            mid[2 * j] = res[:, :NZ]
            mid[2 * j + 1] = res[:, NZ:]

    which = (lax.broadcasted_iota(jnp.int32, (16, 1), 0) // 4)

    def kron_of(dims):
        rep = (
            lax.broadcasted_iota(jnp.int32, (1024, 64), 0) // 16
            == lax.broadcasted_iota(jnp.int32, (1024, 64), 1)
        ).astype(F32).astype(BF16)
        half = dot(rep, pw_ref[...], dims).astype(BF16)
        for m in range(4):
            full = dot(half[256 * m:256 * (m + 1)], rep, ((1,), (1,)))
            same = (
                lax.broadcasted_iota(jnp.int32, (256, 1024), 0) % 16
                == lax.broadcasted_iota(jnp.int32, (256, 1024), 1) % 16
            )
            kron[256 * m:256 * (m + 1), :] = jnp.where(same, full, 0.0).astype(BF16)

    def pointwise(src, with_offset):
        def step(n, c):
            yb, m = n // 4, n % 4
            rows = pl.ds(pl.multiple_of(yb * 16, 16), 16)
            rhs = jnp.concatenate([src[:, x, rows, :].reshape(1024, NZ) for x in range(2)], axis=1)
            res = dot(kron[pl.ds(pl.multiple_of(m * 256, 256), 256), :], rhs)
            for x in range(2):
                part = res[:, x * NZ:(x + 1) * NZ].reshape(16, 2, 8, NZ)
                if with_offset:
                    part = part + offb[pl.ds(m * 16, 16)][:, None]
                loc[pl.ds(m * 16, 16), x, rows, :] = part.reshape(16, 16, NZ)
            return c

        lax.fori_loop(0, 12, step, 0)

    tabs[0].wait()

    def forward(g):
        act_copy(g).wait()
        put_mid(g, dot(by[...], lanes(act, g)))

    for g in range(8):
        forward(g)
    own_w.wait()
    tabs[1].wait()
    pl.semaphore_wait(bar, 70)

    def weights_to(src, owner, half, step):
        pltpu.make_async_remote_copy(
            src.at[pl.ds(2 * half, 2)], wbuf.at[owner, pl.ds(2 * half, 2)], wssem, wrsem.at[owner, half],
            device_id=(zh * 8 + (y + step) % 8, s), device_id_type=MESH,
        ).start()

    def weights_here(owner, half):
        here = wbuf.at[owner, pl.ds(2 * half, 2)]
        pltpu.make_async_copy(here, here, wrsem.at[owner, half]).wait()

    for step in (2, 1):
        for half in range(2):
            weights_to(w_own, y, half, step % 8)
            weights_to(w_own, y, 1 - half, -step % 8)
    z_and_send(fz, send.at[0], 0)

    for t in tabs[2:]:
        t.wait()

    def spread(o, c):
        offb[o] = jnp.full((8, NZ), off_ref[o], F32)
        return c

    lax.fori_loop(0, C, spread, 0)
    kron_of(((1,), (1,)))

    before, behind = (y + 6) % 8, (y + 2) % 8
    for half in range(2):
        weights_here(before, half)
        weights_to(wbuf.at[before], before, half, 1)
        if half == 0:
            weights_to(wbuf.at[before], before, half, 2)
        weights_here(behind, 1 - half)
        weights_to(wbuf.at[behind], behind, 1 - half, 7)
        if half == 0:
            weights_to(wbuf.at[behind], behind, 1 - half, 6)

    landed(0)
    spec[0] = to_modes(0, 1.0).reshape(8, 16, 128)
    share(spec.at[0], xin, 0)

    for n in range(8):
        yy = peer_y(7 - n)
        if n not in (0, 3, 4):
            weights_here(yy, 0)
            weights_here(yy, 1)
        w = (w_own if n == 0 else wbuf.at[yy])[...].reshape(4 * C, 2 * C)
        turned = pltpu.roll(w.astype(F32), 64, 1)
        rows = pl.ds(yy * 4, 4)
        wall[rows, 0:64, :] = w.reshape(4, C, 2 * C)
        wall[rows, 64:128, :] = jnp.where(low, -turned, turned).astype(BF16).reshape(4, C, 2 * C)
        x = spec[0, yy].astype(F32)
        x4 = jnp.concatenate([jnp.where(which == i, x, 0.0) for i in range(4)], axis=1).astype(BF16)
        mix[yy] = dot(x4, wall[rows].reshape(512, 128)).astype(BF16)
    mixed = mix[...].reshape(128, 128)
    back[0] = from_modes(mixed, 1.0 / (NX * NY * NZ)).reshape(64, 4, 128)
    send_back(back.at[0], 1)
    pointwise(act, True)

    landed(1)
    inverse_z(1, fzw)

    def middle(g):
        rows = pl.ds(g * GRP, GRP)
        field = dot(byt[...], get_mid(g))
        halves = []
        for x in range(2):
            value = field[:, x * NZ:(x + 1) * NZ].reshape(GRP, NY, NZ) + loc[rows, x]
            grad = (cot[rows, x].astype(F32) * gelu_slope(value)).astype(BF16)
            slope[rows, x] = grad
            halves.append(grad.reshape(GRP * NY, NZ))
        put_mid(g, dot(by[...], jnp.concatenate(halves, axis=1)))

    for g in range(8):
        middle(g)
    z_and_send(fzw, send.at[1], 2)
    kron_of(((1,), (0,)))

    landed(2)
    spec_grad = to_modes(2, 1.0 / (NX * NY * NZ))
    spec[1] = spec_grad.reshape(8, 16, 128)
    share(spec.at[1], din, 1)
    mixed = []
    for t in range(8):
        res = dot(spec_grad[16 * t:16 * (t + 1)], wall[4 * t:4 * (t + 1)].reshape(512, 128), ((1,), (1,)))
        total = jnp.where(which == 0, res[:, 0:128], 0.0)
        for i in range(1, 4):
            total = total + jnp.where(which == i, res[:, 128 * i:128 * (i + 1)], 0.0)
        mixed.append(total)
    mixed = jnp.concatenate(mixed, axis=0).astype(BF16)
    back[1] = from_modes(mixed, 1.0).reshape(64, 4, 128)
    send_back(back.at[1], 3)
    pointwise(slope, False)

    for k, buf in enumerate((xin, din)):
        pltpu.make_async_copy(buf, buf, xrsem.at[k]).wait()
    left = xin[...].reshape(128, 128).astype(F32)
    right = din[...].reshape(128, 128)
    mode = lax.broadcasted_iota(jnp.int32, (128, 1), 0) // 4 % 4
    for i in range(4):
        g = dot(jnp.where(mode == i, left, 0.0).astype(BF16), right, ((0,), (0,)))
        turned = pltpu.roll(g[64:128], 64, 1)
        gsb[i] = g[0:64] + jnp.where(low, turned, -turned)
    gs_out = pltpu.make_async_copy(gsb, gs_h, w_sem)
    gs_out.start()

    landed(3)
    inverse_z(3, fz)

    def last(g):
        rows = pl.ds(g * GRP, GRP)
        field = dot(byt[...], get_mid(g))
        for x in range(2):
            value = field[:, x * NZ:(x + 1) * NZ].reshape(GRP, NY, NZ) + loc[rows, x]
            outb[rows, x] = value.astype(BF16)
        pltpu.make_async_copy(outb.at[rows], out_h.at[rows], out_sem.at[g]).start()

    for g in range(8):
        last(g)
    for g in range(8):
        rows = pl.ds(g * GRP, GRP)
        pltpu.make_async_copy(outb.at[rows], out_h.at[rows], out_sem.at[g]).wait()
    gs_out.wait()
    for st in range(4):
        sent = land.at[st, pl.ds(0, 63)]
        pltpu.make_async_copy(sent, sent, ssem.at[st]).wait()
    sent = wbuf.at[pl.ds(0, 7)]
    pltpu.make_async_copy(sent, sent, wssem).wait()
    for k in range(2):
        sent = xin.at[pl.ds(0, 7)]
        pltpu.make_async_copy(sent, sent, xssem.at[k]).wait()


def body(activations, cotangent, mode_weights, pointwise, offsets):
    shape = (C, 2, NY, NZ)
    consts = [jnp.asarray(t) for t in tables()]
    hbm = pl.BlockSpec(memory_space=pltpu.HBM)
    grad_in, grad_spectral = pl.pallas_call(
        kernel,
        out_shape=(
            jax.ShapeDtypeStruct(shape, BF16),
            jax.ShapeDtypeStruct((4, C, 2 * C), F32),
        ),
        in_specs=[hbm, hbm, hbm, pl.BlockSpec(memory_space=pltpu.VMEM), pl.BlockSpec(memory_space=pltpu.SMEM)]
        + [hbm] * 6,
        out_specs=(hbm, hbm),
        scratch_shapes=[
            pltpu.VMEM(shape, BF16),
            pltpu.VMEM(shape, BF16),
            pltpu.VMEM((4, C, 2 * C), BF16),
        ]
        + [pltpu.VMEM(t.shape, BF16) for t in consts]
        + [
            pltpu.VMEM((2 * MY, 128, NZ), F32),
            pltpu.VMEM((8, 16, 128), BF16),
            pltpu.VMEM(shape, F32),
            pltpu.VMEM(shape, BF16),
            pltpu.VMEM(shape, BF16),
            pltpu.VMEM((C, 8, NZ), F32),
            pltpu.VMEM((1024, 1024), BF16),
            pltpu.VMEM((32, 128, 128), BF16),
            pltpu.VMEM((8, 4, C, 2 * C), BF16),
            pltpu.VMEM((2, 8, 16, 128), BF16),
            pltpu.VMEM((8, 16, 128), BF16),
            pltpu.VMEM((8, 16, 128), BF16),
            pltpu.VMEM((4, C, 2 * C), F32),
            pltpu.VMEM((2, 64, 4, 128), BF16),
            pltpu.VMEM((2, 64, 4, 128), BF16),
            pltpu.VMEM((4, 64, 4, 128), BF16),
            pltpu.SemaphoreType.DMA((8,)),
            pltpu.SemaphoreType.DMA((7,)),
            pltpu.SemaphoreType.DMA,
            pltpu.SemaphoreType.DMA((8,)),
            pltpu.SemaphoreType.DMA((4,)),
            pltpu.SemaphoreType.DMA((4,)),
            pltpu.SemaphoreType.DMA,
            pltpu.SemaphoreType.DMA((8, 2)),
            pltpu.SemaphoreType.DMA((2,)),
            pltpu.SemaphoreType.DMA((2,)),
        ],
        compiler_params=pltpu.CompilerParams(
            collective_id=0, has_side_effects=True, vmem_limit_bytes=62 << 20
        ),
    )(activations.reshape(shape), cotangent.reshape(shape), mode_weights, pointwise, offsets, *consts)
    return grad_in.reshape(activations.shape), grad_spectral


def solution(mesh):
    return jax.shard_map(
        body,
        mesh=mesh,
        in_specs=(
            P("dp", None, "space", None, None),
            P("dp", None, "space", None, None),
            P(("space", "dp"), None, None),
            P(),
            P(),
        ),
        out_specs=(P("dp", None, "space", None, None), P(("space", "dp"), None, None)),
        check_vma=False,
    )
```

```python
import jax
import jax.numpy as jnp
import numpy as np
from jax import lax
from jax.experimental import pallas as pl
from jax.experimental.pallas import tpu as pltpu
from jax.sharding import PartitionSpec as P

MX, MY, MZ = 16, 16, 8
NX, NY, NZ = 32, 48, 128
C = 64
GRP = 8
MESH = pl.DeviceIdType.MESH
F32, BF16 = jnp.float32, jnp.bfloat16


def centered(count):
    index = np.arange(count)
    return np.where(index < count // 2, index, index - count)


def tables():
    ty = 2 * np.pi * centered(MY)[:, None] * np.arange(NY)[None, :] / NY
    along_y = np.stack([np.cos(ty), -np.sin(ty)], 1)
    eye = np.eye(GRP)
    to_y = np.einsum("jry,cd->jrcdy", along_y, eye).reshape(MY * 2 * GRP, GRP * NY)
    tz = 2 * np.pi * np.arange(MZ)[:, None] * np.arange(NZ)[None, :] / NZ
    along_z = np.zeros((MZ, 2, 2, NZ))
    along_z[:, 0, 0], along_z[:, 0, 1] = np.cos(tz), np.sin(tz)
    along_z[:, 1, 0], along_z[:, 1, 1] = -np.sin(tz), np.cos(tz)
    weight = np.where(np.arange(MZ) == 0, 1.0, 2.0)[:, None, None, None]
    plain = along_z.reshape(MZ * 2, 2 * NZ)
    weighted = (along_z * weight).reshape(MZ * 2, 2 * NZ)
    s = 2 * np.pi * centered(MX)[None, :] * np.arange(NX)[:, None] / NX
    line = np.zeros((NX, 2, MX, 2))
    line[:, 0, :, 0], line[:, 0, :, 1] = np.cos(s), -np.sin(s)
    line[:, 1, :, 0], line[:, 1, :, 1] = np.sin(s), np.cos(s)
    line = line.reshape(NX // 2, 2, 2, MX, 2)
    to_q = np.einsum("shuqa,bd,ke->hakqbdseu", line, np.eye(4), np.eye(2)).reshape(512, 256)
    to_x = np.einsum("shuqa,bd,ke->habskueqd", line, np.eye(4), np.eye(2)).reshape(1024, 128)
    cast = lambda t: np.asarray(t.astype(np.float32)).astype(jnp.bfloat16)
    return tuple(cast(t) for t in (to_y, to_y.T.copy(), plain, weighted, to_q, to_x))


def dot(a, b, dims=((1,), (0,))):
    return lax.dot_general(a, b, (dims, ((), ())), preferred_element_type=F32)


def gelu_slope(value):
    cdf = 0.5 * (1.0 + lax.erf(value * 0.7071067811865476))
    density = jnp.exp(-0.5 * value * value) * 0.3989422804014327
    return cdf + value * density


def kernel(
    act_h, cot_h, w_h, pw_h, off_h, by_h, byt_h, fz_h, fzw_h, bq_h, bx_h,
    out_h, gs_h,
    act, cot, w_own, pw_ref, off_ref, by, byt, fz, fzw, bq, bx,
    mid, mix, loc, slope, outb, offb, kron, wall, wbuf, spec, xin, din, gsb,
    send, back, land,
    in_sem, tab_sem, w_sem, out_sem, ssem, rsem, wssem, wrsem, xssem, xrsem,
):
    dp = lax.axis_index("dp")
    s = lax.axis_index("space")
    zh, y = dp // 8, dp % 8
    me = zh * 16 + s
    low = lax.broadcasted_iota(jnp.int32, (1, 128), 1) < 64

    def far_first(k, half):
        return half + (1 - 2 * (k % 2)) * ((k + 1) // 2)

    z = 2 * zh + lax.rem(lax.div(s, 2), 2)
    zts = [lax.rem(z + k, 8) for k in range(8)]
    zhs = [lax.div(zt, 2) for zt in zts]
    xts = [lax.rem(lax.div(s, 4) + k, 4) * 4 for k in range(4)]
    slabs = [[xt + lax.rem(zt, 2) * 2 for xt in xts] for zt in zts]
    cores = [lax.rem(s, 2), lax.rem(s + 1, 2)]
    yys = [lax.rem(y + far_first(k, 4), 8) for k in range(8)]
    order = sorted(
        ((dz, dx, dc) for dz in range(8) for dx in range(4) for dc in range(2)),
        key=lambda d: (-min(d[0], 8 - d[0]) - min(d[1], 4 - d[1]), -d[2]),
    )

    def peer(n):
        dz, dx, dc = order[n]
        return zhs[dz], slabs[dz][dx] + cores[dc]

    def peer_y(n):
        return yys[n]

    bar = pltpu.get_barrier_semaphore()
    for n in range(63):
        zt, st = peer(n)
        pl.semaphore_signal(bar, inc=1, device_id=(zt * 8 + y, st), device_id_type=MESH)
    for n in range(7):
        pl.semaphore_signal(bar, inc=1, device_id=(zh * 8 + peer_y(n), s), device_id_type=MESH)

    def act_copy(g):
        rows = pl.ds(g * GRP, GRP)
        return pltpu.make_async_copy(act_h.at[rows], act.at[rows], in_sem.at[g])

    tabs = [
        pltpu.make_async_copy(h, v, tab_sem.at[i])
        for i, (h, v) in enumerate(
            ((by_h, by), (fz_h, fz), (bq_h, bq), (bx_h, bx), (byt_h, byt), (fzw_h, fzw), (pw_h, pw_ref), (off_h, off_ref), (cot_h, cot))
        )
    ]
    own_w = pltpu.make_async_copy(w_h, w_own, w_sem)
    tabs[0].start()
    for g in range(8):
        act_copy(g).start()
    own_w.start()
    for t in tabs[1:]:
        t.start()

    def lanes(ref, g):
        rows = pl.ds(g * GRP, GRP)
        return jnp.concatenate(
            [ref[rows, x].reshape(GRP * NY, NZ) for x in range(2)], axis=1
        )

    def put_mid(g, res):
        for x in range(2):
            rows = pl.ds(x * 64 + g * GRP, GRP)
            mid[:, rows, :] = res[:, x * NZ:(x + 1) * NZ].reshape(2 * MY, GRP, NZ)

    def get_mid(g):
        parts = []
        for x in range(2):
            rows = pl.ds(x * 64 + g * GRP, GRP)
            parts.append(mid[:, rows, :].reshape(2 * MY * GRP, NZ).astype(BF16))
        return jnp.concatenate(parts, axis=1)

    def forward_z(table, sbuf):
        for j in range(16):
            pair = jnp.concatenate([mid[2 * j].astype(BF16), mid[2 * j + 1].astype(BF16)], axis=1)
            res = dot(table[...], pair, ((1,), (1,)))
            sbuf[4 * j:4 * (j + 1)] = res.astype(BF16).reshape(4, 4, 128)

    def exchange(sbuf, st, to_owner):
        slot = me if to_owner else s * 4 + zh
        for n in range(64):
            zt, xt = peer(n)
            block = sbuf.at[xt * 4 + zt] if to_owner else sbuf.at[zt * 16 + xt]
            if n == 63:
                pltpu.make_async_copy(block, land.at[st, slot], rsem.at[st]).start()
            else:
                pltpu.make_async_remote_copy(
                    block, land.at[st, slot], ssem.at[st], rsem.at[st],
                    device_id=(zt * 8 + y, xt), device_id_type=MESH,
                ).start()

    def landed(st):
        whole = land.at[st]
        pltpu.make_async_copy(whole, whole, rsem.at[st]).wait()

    def share(src, dst, k):
        for n in range(7):
            yy = peer_y(n)
            pltpu.make_async_remote_copy(
                src.at[yy], dst.at[y], xssem.at[k], xrsem.at[k],
                device_id=(zh * 8 + yy, s), device_id_type=MESH,
            ).start()
        pltpu.make_async_copy(src.at[y], dst.at[y], xrsem.at[k]).start()

    def to_modes(st, scale):
        r = dot(bq[...], land[st].reshape(256, 128))
        first = jnp.where(low, r[0:128], r[384:512])
        second = jnp.where(low, r[128:256], r[256:384])
        return ((first + pltpu.roll(second, 64, 1)) * scale).astype(BF16)

    def from_modes(mixed, scale):
        r = dot(bx[...], mixed)
        first = jnp.where(low, r[0:256], r[768:1024])
        second = jnp.where(low, r[512:768], r[256:512])
        return ((first + pltpu.roll(second, 64, 1)) * scale).astype(BF16)

    def inverse_z(st, table):
        rows = land[st].reshape(256, 128)
        for j in range(16):
            res = dot(rows[16 * j:16 * (j + 1)], table[...], ((0,), (0,)))
            mid[2 * j] = res[:, :NZ]
            mid[2 * j + 1] = res[:, NZ:]

    which = (lax.broadcasted_iota(jnp.int32, (16, 1), 0) // 4)

    def kron_of(dims):
        rep = (
            lax.broadcasted_iota(jnp.int32, (1024, 64), 0) // 16
            == lax.broadcasted_iota(jnp.int32, (1024, 64), 1)
        ).astype(F32).astype(BF16)
        half = dot(rep, pw_ref[...], dims).astype(BF16)
        for m in range(4):
            full = dot(half[256 * m:256 * (m + 1)], rep, ((1,), (1,)))
            same = (
                lax.broadcasted_iota(jnp.int32, (256, 1024), 0) % 16
                == lax.broadcasted_iota(jnp.int32, (256, 1024), 1) % 16
            )
            kron[256 * m:256 * (m + 1), :] = jnp.where(same, full, 0.0).astype(BF16)

    def pointwise(src, with_offset, parts):
        def step(n, c):
            yb, m = n // 4, n % 4
            rows = pl.ds(pl.multiple_of(yb * 16, 16), 16)
            rhs = jnp.concatenate([src[:, x, rows, :].reshape(1024, NZ) for x in range(2)], axis=1)
            res = dot(kron[pl.ds(pl.multiple_of(m * 256, 256), 256), :], rhs)
            for x in range(2):
                part = res[:, x * NZ:(x + 1) * NZ].reshape(16, 2, 8, NZ)
                if with_offset:
                    part = part + offb[pl.ds(m * 16, 16)][:, None]
                loc[pl.ds(m * 16, 16), x, rows, :] = part.reshape(16, 16, NZ)
            return c

        lax.fori_loop(4 * parts[0], 4 * parts[1], step, 0)

    tabs[0].wait()

    def forward(g):
        act_copy(g).wait()
        put_mid(g, dot(by[...], lanes(act, g)))

    for g in range(8):
        forward(g)
    own_w.wait()
    tabs[1].wait()
    forward_z(fz, send.at[0])
    pl.semaphore_wait(bar, 70)

    def weights_to(src, owner, half, step):
        pltpu.make_async_remote_copy(
            src.at[pl.ds(2 * half, 2)], wbuf.at[owner, pl.ds(2 * half, 2)], wssem, wrsem.at[owner, half],
            device_id=(zh * 8 + (y + step) % 8, s), device_id_type=MESH,
        ).start()

    def weights_here(owner, half):
        here = wbuf.at[owner, pl.ds(2 * half, 2)]
        pltpu.make_async_copy(here, here, wrsem.at[owner, half]).wait()

    for step in (2, 1):
        for half in range(2):
            weights_to(w_own, y, half, step % 8)
            weights_to(w_own, y, 1 - half, -step % 8)
    exchange(send.at[0], 0, True)

    for t in tabs[2:]:
        t.wait()

    def spread(o, c):
        offb[o] = jnp.full((8, NZ), off_ref[o], F32)
        return c

    lax.fori_loop(0, C, spread, 0)
    kron_of(((1,), (1,)))

    before, behind = (y + 6) % 8, (y + 2) % 8
    for half in range(2):
        weights_here(before, half)
        weights_to(wbuf.at[before], before, half, 1)
        if half == 0:
            weights_to(wbuf.at[before], before, half, 2)
        weights_here(behind, 1 - half)
        weights_to(wbuf.at[behind], behind, 1 - half, 7)
        if half == 0:
            weights_to(wbuf.at[behind], behind, 1 - half, 6)

    pointwise(act, True, (0, 1))
    landed(0)
    spec[0] = to_modes(0, 1.0).reshape(8, 16, 128)
    share(spec.at[0], xin, 0)

    for n in range(8):
        yy = peer_y(7 - n)
        if n not in (0, 3, 4):
            weights_here(yy, 0)
            weights_here(yy, 1)
        w = (w_own if n == 0 else wbuf.at[yy])[...].reshape(4 * C, 2 * C)
        turned = pltpu.roll(w.astype(F32), 64, 1)
        rows = pl.ds(yy * 4, 4)
        wall[rows, 0:64, :] = w.reshape(4, C, 2 * C)
        wall[rows, 64:128, :] = jnp.where(low, -turned, turned).astype(BF16).reshape(4, C, 2 * C)
        x = spec[0, yy].astype(F32)
        x4 = jnp.concatenate([jnp.where(which == i, x, 0.0) for i in range(4)], axis=1).astype(BF16)
        mix[yy] = dot(x4, wall[rows].reshape(512, 128)).astype(BF16)
    mixed = mix[...].reshape(128, 128)
    back[0] = from_modes(mixed, 1.0 / (NX * NY * NZ)).reshape(64, 4, 128)
    exchange(back.at[0], 1, False)
    pointwise(act, True, (1, 3))

    landed(1)
    inverse_z(1, fzw)

    def middle(g):
        rows = pl.ds(g * GRP, GRP)
        field = dot(byt[...], get_mid(g))
        halves = []
        for x in range(2):
            value = field[:, x * NZ:(x + 1) * NZ].reshape(GRP, NY, NZ) + loc[rows, x]
            grad = (cot[rows, x].astype(F32) * gelu_slope(value)).astype(BF16)
            slope[rows, x] = grad
            halves.append(grad.reshape(GRP * NY, NZ))
        put_mid(g, dot(by[...], jnp.concatenate(halves, axis=1)))

    for g in range(8):
        middle(g)
    forward_z(fzw, send.at[1])
    exchange(send.at[1], 2, True)
    kron_of(((1,), (0,)))
    pointwise(slope, False, (0, 1))

    landed(2)
    spec_grad = to_modes(2, 1.0 / (NX * NY * NZ))
    spec[1] = spec_grad.reshape(8, 16, 128)
    share(spec.at[1], din, 1)
    mixed = []
    for t in range(8):
        res = dot(spec_grad[16 * t:16 * (t + 1)], wall[4 * t:4 * (t + 1)].reshape(512, 128), ((1,), (1,)))
        total = jnp.where(which == 0, res[:, 0:128], 0.0)
        for i in range(1, 4):
            total = total + jnp.where(which == i, res[:, 128 * i:128 * (i + 1)], 0.0)
        mixed.append(total)
    mixed = jnp.concatenate(mixed, axis=0).astype(BF16)
    back[1] = from_modes(mixed, 1.0).reshape(64, 4, 128)
    exchange(back.at[1], 3, False)
    pointwise(slope, False, (1, 3))

    for k, buf in enumerate((xin, din)):
        pltpu.make_async_copy(buf, buf, xrsem.at[k]).wait()
    left = xin[...].reshape(128, 128).astype(F32)
    right = din[...].reshape(128, 128)
    mode = lax.broadcasted_iota(jnp.int32, (128, 1), 0) // 4 % 4
    for i in range(4):
        g = dot(jnp.where(mode == i, left, 0.0).astype(BF16), right, ((0,), (0,)))
        turned = pltpu.roll(g[64:128], 64, 1)
        gsb[i] = g[0:64] + jnp.where(low, turned, -turned)
    gs_out = pltpu.make_async_copy(gsb, gs_h, w_sem)
    gs_out.start()

    landed(3)
    inverse_z(3, fz)

    def last(g):
        rows = pl.ds(g * GRP, GRP)
        field = dot(byt[...], get_mid(g))
        for x in range(2):
            value = field[:, x * NZ:(x + 1) * NZ].reshape(GRP, NY, NZ) + loc[rows, x]
            outb[rows, x] = value.astype(BF16)
        pltpu.make_async_copy(outb.at[rows], out_h.at[rows], out_sem.at[g]).start()

    for g in range(8):
        last(g)
    for g in range(8):
        rows = pl.ds(g * GRP, GRP)
        pltpu.make_async_copy(outb.at[rows], out_h.at[rows], out_sem.at[g]).wait()
    gs_out.wait()
    for st in range(4):
        sent = land.at[st, pl.ds(0, 63)]
        pltpu.make_async_copy(sent, sent, ssem.at[st]).wait()
    sent = wbuf.at[pl.ds(0, 7)]
    pltpu.make_async_copy(sent, sent, wssem).wait()
    for k in range(2):
        sent = xin.at[pl.ds(0, 7)]
        pltpu.make_async_copy(sent, sent, xssem.at[k]).wait()


def body(activations, cotangent, mode_weights, pointwise, offsets):
    shape = (C, 2, NY, NZ)
    consts = [jnp.asarray(t) for t in tables()]
    operands = (activations.reshape(shape), cotangent.reshape(shape), mode_weights, pointwise, offsets, *consts)
    hbm = pl.BlockSpec(memory_space=pltpu.HBM)
    grad_in, grad_spectral = pl.pallas_call(
        kernel,
        out_shape=(
            jax.ShapeDtypeStruct(shape, BF16),
            jax.ShapeDtypeStruct((4, C, 2 * C), F32),
        ),
        in_specs=[hbm] * 11,
        out_specs=(pl.BlockSpec(memory_space=pl.ANY),) * 2,
        scratch_shapes=[
            pltpu.VMEM(shape, BF16),
            pltpu.VMEM(shape, BF16),
            pltpu.VMEM((4, C, 2 * C), BF16),
            pltpu.VMEM((C, C), BF16),
            pltpu.SMEM((C,), F32),
        ]
        + [pltpu.VMEM(t.shape, BF16) for t in consts]
        + [
            pltpu.VMEM((2 * MY, 128, NZ), F32),
            pltpu.VMEM((8, 16, 128), BF16),
            pltpu.VMEM(shape, F32),
            pltpu.VMEM(shape, BF16),
            pltpu.VMEM(shape, BF16),
            pltpu.VMEM((C, 8, NZ), F32),
            pltpu.VMEM((1024, 1024), BF16),
            pltpu.VMEM((32, 128, 128), BF16),
            pltpu.VMEM((8, 4, C, 2 * C), BF16),
            pltpu.VMEM((2, 8, 16, 128), BF16),
            pltpu.VMEM((8, 16, 128), BF16),
            pltpu.VMEM((8, 16, 128), BF16),
            pltpu.VMEM((4, C, 2 * C), F32),
            pltpu.VMEM((2, 64, 4, 128), BF16),
            pltpu.VMEM((2, 64, 4, 128), BF16),
            pltpu.VMEM((4, 64, 4, 128), BF16),
            pltpu.SemaphoreType.DMA((8,)),
            pltpu.SemaphoreType.DMA((9,)),
            pltpu.SemaphoreType.DMA,
            pltpu.SemaphoreType.DMA((8,)),
            pltpu.SemaphoreType.DMA((4,)),
            pltpu.SemaphoreType.DMA((4,)),
            pltpu.SemaphoreType.DMA,
            pltpu.SemaphoreType.DMA((8, 2)),
            pltpu.SemaphoreType.DMA((2,)),
            pltpu.SemaphoreType.DMA((2,)),
        ],
        compiler_params=pltpu.CompilerParams(
            collective_id=0, has_side_effects=True, vmem_limit_bytes=32 << 20
        ),
    )(*(pltpu.with_memory_space_constraint(a, pltpu.HBM) for a in operands))
    return grad_in.reshape(activations.shape), grad_spectral


def solution(mesh):
    return jax.shard_map(
        body,
        mesh=mesh,
        in_specs=(
            P("dp", None, "space", None, None),
            P("dp", None, "space", None, None),
            P(("space", "dp"), None, None),
            P(),
            P(),
        ),
        out_specs=(P("dp", None, "space", None, None), P(("space", "dp"), None, None)),
        check_vma=False,
    )
```

```python
import jax
import jax.numpy as jnp
import numpy as np
from jax import lax
from jax.experimental import pallas as pl
from jax.experimental.pallas import tpu as pltpu
from jax.sharding import PartitionSpec as P

MX, MY, MZ = 16, 16, 8
NX, NY, NZ = 32, 48, 128
C = 64
GRP = 8
MESH = pl.DeviceIdType.MESH
F32, BF16 = jnp.float32, jnp.bfloat16


def centered(count):
    index = np.arange(count)
    return np.where(index < count // 2, index, index - count)


def tables():
    ty = 2 * np.pi * centered(MY)[:, None] * np.arange(NY)[None, :] / NY
    along_y = np.stack([np.cos(ty), -np.sin(ty)], 1)
    eye = np.eye(GRP)
    to_y = np.einsum("jry,cd->jrcdy", along_y, eye).reshape(MY * 2 * GRP, GRP * NY)
    tz = 2 * np.pi * np.arange(MZ)[:, None] * np.arange(NZ)[None, :] / NZ
    along_z = np.zeros((MZ, 2, 2, NZ))
    along_z[:, 0, 0], along_z[:, 0, 1] = np.cos(tz), np.sin(tz)
    along_z[:, 1, 0], along_z[:, 1, 1] = -np.sin(tz), np.cos(tz)
    weight = np.where(np.arange(MZ) == 0, 1.0, 2.0)[:, None, None, None]
    plain = along_z.reshape(MZ * 2, 2 * NZ)
    weighted = (along_z * weight).reshape(MZ * 2, 2 * NZ)
    s = 2 * np.pi * centered(MX)[None, :] * np.arange(NX)[:, None] / NX
    line = np.zeros((NX, 2, MX, 2))
    line[:, 0, :, 0], line[:, 0, :, 1] = np.cos(s), -np.sin(s)
    line[:, 1, :, 0], line[:, 1, :, 1] = np.sin(s), np.cos(s)
    line = line.reshape(NX // 2, 2, 2, MX, 2)
    to_q = np.einsum("shuqa,bd,ke->hakqbdseu", line, np.eye(4), np.eye(2)).reshape(512, 256)
    to_x = np.einsum("shuqa,bd,ke->hbskuaeqd", line, np.eye(4), np.eye(2)).reshape(512, 256)
    cast = lambda t: np.asarray(t.astype(np.float32)).astype(jnp.bfloat16)
    return tuple(cast(t) for t in (to_y, to_y.T.copy(), plain, weighted, to_q, to_x))


def dot(a, b, dims=((1,), (0,))):
    return lax.dot_general(a, b, (dims, ((), ())), preferred_element_type=F32)


def gelu_slope(value):
    cdf = 0.5 * (1.0 + lax.erf(value * 0.7071067811865476))
    density = jnp.exp(-0.5 * value * value) * 0.3989422804014327
    return cdf + value * density


def get_mid(mid, g):
    parts = []
    for x in range(2):
        rows = pl.ds(x * 64 + g * GRP, GRP)
        parts.append(mid[:, rows, :].reshape(2 * MY * GRP, NZ).astype(BF16))
    return jnp.concatenate(parts, axis=1)


def last_kernel(mid, loc, gsb, byt, out_h, gs_h, outb, sem):
    gs_out = pltpu.make_async_copy(gsb, gs_h, sem.at[8])
    gs_out.start()
    copies = []
    for g in range(8):
        rows = pl.ds(g * GRP, GRP)
        field = dot(byt[...], get_mid(mid, g))
        for x in range(2):
            value = field[:, x * NZ:(x + 1) * NZ].reshape(GRP, NY, NZ) + loc[rows, x]
            outb[rows, x] = value.astype(BF16)
        copies.append(pltpu.make_async_copy(outb.at[rows], out_h.at[rows], sem.at[g]))
        copies[g].start()
    for copy in copies + [gs_out]:
        copy.wait()


def kernel(
    act_h, cot_h, w_h, pw_h, off_h, by_h, byt_h, fz_h, fzw_h, bq_h, bx_h,
    mid, loc, gsb, byt,
    act, cot, w_own, pw_ref, off_ref, by, fz, fzw, bq, bx,
    mix, slope, offb, kron, wall, wbuf, spec, xin, din,
    send, back, land,
    in_sem, tab_sem, w_sem, ssem, rsem, wssem, wrsem, xssem, xrsem,
):
    dp = lax.axis_index("dp")
    s = lax.axis_index("space")
    zh, y = dp // 8, dp % 8
    me = zh * 16 + s
    low = lax.broadcasted_iota(jnp.int32, (1, 128), 1) < 64

    def far_first(k, half):
        return half + (1 - 2 * (k % 2)) * ((k + 1) // 2)

    z = 2 * zh + lax.rem(lax.div(s, 2), 2)
    zts = [lax.rem(z + k, 8) for k in range(8)]
    zhs = [lax.div(zt, 2) for zt in zts]
    xts = [lax.rem(lax.div(s, 4) + k, 4) * 4 for k in range(4)]
    slabs = [[xt + lax.rem(zt, 2) * 2 for xt in xts] for zt in zts]
    cores = [lax.rem(s, 2), lax.rem(s + 1, 2)]
    yys = [lax.rem(y + far_first(k, 4), 8) for k in range(8)]
    order = sorted(
        ((dz, dx, dc) for dz in range(8) for dx in range(4) for dc in range(2)),
        key=lambda d: (-min(d[0], 8 - d[0]) - min(d[1], 4 - d[1]), -d[2]),
    )

    def peer(n):
        dz, dx, dc = order[n]
        return zhs[dz], slabs[dz][dx] + cores[dc]

    def peer_y(n):
        return yys[n]

    bar = pltpu.get_barrier_semaphore()
    for n in range(63):
        zt, st = peer(n)
        pl.semaphore_signal(bar, inc=1, device_id=(zt * 8 + y, st), device_id_type=MESH)
    for n in range(7):
        pl.semaphore_signal(bar, inc=1, device_id=(zh * 8 + peer_y(n), s), device_id_type=MESH)

    def act_copy(g):
        rows = pl.ds(g * GRP, GRP)
        return pltpu.make_async_copy(act_h.at[rows], act.at[rows], in_sem.at[g])

    tabs = [
        pltpu.make_async_copy(h, v, tab_sem.at[i])
        for i, (h, v) in enumerate(
            ((by_h, by), (fz_h, fz), (bq_h, bq), (bx_h, bx), (byt_h, byt), (fzw_h, fzw), (pw_h, pw_ref), (off_h, off_ref), (cot_h, cot))
        )
    ]
    own_w = pltpu.make_async_copy(w_h, w_own, w_sem)
    tabs[0].start()
    for g in range(8):
        act_copy(g).start()
    own_w.start()
    for t in tabs[1:]:
        t.start()

    def lanes(ref, g):
        rows = pl.ds(g * GRP, GRP)
        return jnp.concatenate(
            [ref[rows, x].reshape(GRP * NY, NZ) for x in range(2)], axis=1
        )

    def put_mid(g, res):
        for x in range(2):
            rows = pl.ds(x * 64 + g * GRP, GRP)
            mid[:, rows, :] = res[:, x * NZ:(x + 1) * NZ].reshape(2 * MY, GRP, NZ)

    def forward_z(table, sbuf):
        for j in range(16):
            pair = jnp.concatenate([mid[2 * j].astype(BF16), mid[2 * j + 1].astype(BF16)], axis=1)
            res = dot(table[...], pair, ((1,), (1,)))
            sbuf[4 * j:4 * (j + 1)] = res.astype(BF16).reshape(4, 4, 128)

    def exchange(sbuf, st, to_owner):
        slot = me if to_owner else s * 4 + zh
        for n in range(64):
            zt, xt = peer(n)
            block = sbuf.at[xt * 4 + zt] if to_owner else sbuf.at[zt * 16 + xt]
            if n == 63:
                pltpu.make_async_copy(block, land.at[st, slot], rsem.at[st]).start()
            else:
                pltpu.make_async_remote_copy(
                    block, land.at[st, slot], ssem.at[st], rsem.at[st],
                    device_id=(zt * 8 + y, xt), device_id_type=MESH,
                ).start()

    def landed(st):
        whole = land.at[st]
        pltpu.make_async_copy(whole, whole, rsem.at[st]).wait()

    def share(src, dst, k):
        for n in range(7):
            yy = peer_y(n)
            pltpu.make_async_remote_copy(
                src.at[yy], dst.at[y], xssem.at[k], xrsem.at[k],
                device_id=(zh * 8 + yy, s), device_id_type=MESH,
            ).start()
        pltpu.make_async_copy(src.at[y], dst.at[y], xrsem.at[k]).start()

    def to_modes(st, scale):
        r = dot(bq[...], land[st].reshape(256, 128))
        first = jnp.where(low, r[0:128], r[384:512])
        second = jnp.where(low, r[128:256], r[256:384])
        return ((first + pltpu.roll(second, 64, 1)) * scale).astype(BF16)

    def from_modes(mixed, turned, scale):
        first = dot(bx[0:256], jnp.concatenate([mixed, turned], axis=0))
        second = dot(bx[256:512], jnp.concatenate([turned, mixed], axis=0))
        return (jnp.where(low, first, second) * scale).astype(BF16)

    def inverse_z(st, table):
        rows = land[st].reshape(256, 128)
        for j in range(16):
            res = dot(rows[16 * j:16 * (j + 1)], table[...], ((0,), (0,)))
            mid[2 * j] = res[:, :NZ]
            mid[2 * j + 1] = res[:, NZ:]

    which = (lax.broadcasted_iota(jnp.int32, (16, 1), 0) // 4)

    def kron_of(dims):
        rep = (
            lax.broadcasted_iota(jnp.int32, (1024, 64), 0) // 16
            == lax.broadcasted_iota(jnp.int32, (1024, 64), 1)
        ).astype(F32).astype(BF16)
        half = dot(rep, pw_ref[...], dims).astype(BF16)
        for m in range(4):
            full = dot(half[256 * m:256 * (m + 1)], rep, ((1,), (1,)))
            same = (
                lax.broadcasted_iota(jnp.int32, (256, 1024), 0) % 16
                == lax.broadcasted_iota(jnp.int32, (256, 1024), 1) % 16
            )
            kron[256 * m:256 * (m + 1), :] = jnp.where(same, full, 0.0).astype(BF16)

    def pointwise(src, with_offset, parts):
        def step(n, c):
            yb, m = n // 4, n % 4
            rows = pl.ds(pl.multiple_of(yb * 16, 16), 16)
            rhs = jnp.concatenate([src[:, x, rows, :].reshape(1024, NZ) for x in range(2)], axis=1)
            res = dot(kron[pl.ds(pl.multiple_of(m * 256, 256), 256), :], rhs)
            for x in range(2):
                part = res[:, x * NZ:(x + 1) * NZ].reshape(16, 2, 8, NZ)
                if with_offset:
                    part = part + offb[pl.ds(m * 16, 16)][:, None]
                loc[pl.ds(m * 16, 16), x, rows, :] = part.reshape(16, 16, NZ)
            return c

        lax.fori_loop(4 * parts[0], 4 * parts[1], step, 0)

    tabs[0].wait()

    def forward(g):
        act_copy(g).wait()
        put_mid(g, dot(by[...], lanes(act, g)))

    for g in range(8):
        forward(g)
    own_w.wait()
    tabs[1].wait()
    forward_z(fz, send.at[0])
    pl.semaphore_wait(bar, 70)

    def weights_to(src, owner, half, step):
        pltpu.make_async_remote_copy(
            src.at[pl.ds(2 * half, 2)], wbuf.at[owner, pl.ds(2 * half, 2)], wssem, wrsem.at[owner, half],
            device_id=(zh * 8 + (y + step) % 8, s), device_id_type=MESH,
        ).start()

    def weights_here(owner, half):
        here = wbuf.at[owner, pl.ds(2 * half, 2)]
        pltpu.make_async_copy(here, here, wrsem.at[owner, half]).wait()

    for step in (2, 1):
        for half in range(2):
            weights_to(w_own, y, half, step % 8)
            weights_to(w_own, y, 1 - half, -step % 8)
    exchange(send.at[0], 0, True)

    for t in tabs[2:]:
        t.wait()

    def spread(o, c):
        offb[o] = jnp.full((8, NZ), off_ref[o], F32)
        return c

    lax.fori_loop(0, C, spread, 0)
    kron_of(((1,), (1,)))

    before, behind = (y + 6) % 8, (y + 2) % 8
    for half in range(2):
        weights_here(before, half)
        weights_to(wbuf.at[before], before, half, 1)
        if half == 0:
            weights_to(wbuf.at[before], before, half, 2)
        weights_here(behind, 1 - half)
        weights_to(wbuf.at[behind], behind, 1 - half, 7)
        if half == 0:
            weights_to(wbuf.at[behind], behind, 1 - half, 6)

    pointwise(act, True, (0, 1))
    landed(0)
    spec[0] = to_modes(0, 1.0).reshape(8, 16, 128)
    share(spec.at[0], xin, 0)

    for n in range(8):
        yy = peer_y(7 - n)
        if n not in (0, 3, 4):
            weights_here(yy, 0)
            weights_here(yy, 1)
        w = (w_own if n == 0 else wbuf.at[yy])[...].reshape(4 * C, 2 * C)
        turned = pltpu.roll(w.astype(F32), 64, 1)
        rows = pl.ds(yy * 4, 4)
        wall[rows, 0:64, :] = w.reshape(4, C, 2 * C)
        wall[rows, 64:128, :] = jnp.where(low, -turned, turned).astype(BF16).reshape(4, C, 2 * C)
        x = spec[0, yy].astype(F32)
        x4 = jnp.concatenate([jnp.where(which == i, x, 0.0) for i in range(4)], axis=1).astype(BF16)
        res = dot(x4, wall[rows].reshape(512, 128))
        mix[0, yy] = res.astype(BF16)
        mix[1, yy] = pltpu.roll(res, 64, 1).astype(BF16)
    mixed = [mix[i].reshape(128, 128) for i in range(2)]
    back[0] = from_modes(*mixed, 1.0 / (NX * NY * NZ)).reshape(64, 4, 128)
    exchange(back.at[0], 1, False)
    pointwise(act, True, (1, 3))

    landed(1)
    inverse_z(1, fzw)

    def middle(g):
        rows = pl.ds(g * GRP, GRP)
        field = dot(byt[...], get_mid(mid, g))
        halves = []
        for x in range(2):
            value = field[:, x * NZ:(x + 1) * NZ].reshape(GRP, NY, NZ) + loc[rows, x]
            grad = (cot[rows, x].astype(F32) * gelu_slope(value)).astype(BF16)
            slope[rows, x] = grad
            halves.append(grad.reshape(GRP * NY, NZ))
        put_mid(g, dot(by[...], jnp.concatenate(halves, axis=1)))

    for g in range(8):
        middle(g)
    forward_z(fzw, send.at[1])
    exchange(send.at[1], 2, True)
    kron_of(((1,), (0,)))
    pointwise(slope, False, (0, 1))

    landed(2)
    spec_grad = to_modes(2, 1.0 / (NX * NY * NZ))
    spec[1] = spec_grad.reshape(8, 16, 128)
    share(spec.at[1], din, 1)
    mixed = []
    for t in range(8):
        res = dot(spec_grad[16 * t:16 * (t + 1)], wall[4 * t:4 * (t + 1)].reshape(512, 128), ((1,), (1,)))
        total = jnp.where(which == 0, res[:, 0:128], 0.0)
        for i in range(1, 4):
            total = total + jnp.where(which == i, res[:, 128 * i:128 * (i + 1)], 0.0)
        mixed.append(total)
    mixed = jnp.concatenate(mixed, axis=0)
    turned = pltpu.roll(mixed, 64, 1).astype(BF16)
    back[1] = from_modes(mixed.astype(BF16), turned, 1.0).reshape(64, 4, 128)
    exchange(back.at[1], 3, False)
    pointwise(slope, False, (1, 3))

    for k, buf in enumerate((xin, din)):
        pltpu.make_async_copy(buf, buf, xrsem.at[k]).wait()
    left = xin[...].reshape(128, 128).astype(F32)
    right = din[...].reshape(128, 128)
    mode = lax.broadcasted_iota(jnp.int32, (128, 1), 0) // 4 % 4
    for i in range(4):
        g = dot(jnp.where(mode == i, left, 0.0).astype(BF16), right, ((0,), (0,)))
        turned = pltpu.roll(g[64:128], 64, 1)
        gsb[i] = g[0:64] + jnp.where(low, turned, -turned)

    landed(3)
    inverse_z(3, fz)
    for st in range(4):
        sent = land.at[st, pl.ds(0, 63)]
        pltpu.make_async_copy(sent, sent, ssem.at[st]).wait()
    sent = wbuf.at[pl.ds(0, 7)]
    pltpu.make_async_copy(sent, sent, wssem).wait()
    for k in range(2):
        sent = xin.at[pl.ds(0, 7)]
        pltpu.make_async_copy(sent, sent, xssem.at[k]).wait()


def body(activations, cotangent, mode_weights, pointwise, offsets):
    shape = (C, 2, NY, NZ)
    consts = [jnp.asarray(t) for t in tables()]
    operands = (activations.reshape(shape), cotangent.reshape(shape), mode_weights, pointwise, offsets, *consts)
    hbm = pl.BlockSpec(memory_space=pltpu.HBM)
    vmem = pl.BlockSpec(memory_space=pltpu.VMEM)
    handed = pl.pallas_call(
        kernel,
        out_shape=(
            jax.ShapeDtypeStruct((2 * MY, 128, NZ), F32),
            jax.ShapeDtypeStruct(shape, F32),
            jax.ShapeDtypeStruct((4, C, 2 * C), F32),
            jax.ShapeDtypeStruct(consts[1].shape, BF16),
        ),
        in_specs=[hbm] * 11,
        out_specs=(vmem,) * 4,
        scratch_shapes=[
            pltpu.VMEM(shape, BF16),
            pltpu.VMEM(shape, BF16),
            pltpu.VMEM((4, C, 2 * C), BF16),
            pltpu.VMEM((C, C), BF16),
            pltpu.SMEM((C,), F32),
        ]
        + [pltpu.VMEM(t.shape, BF16) for t in consts[:1] + consts[2:]]
        + [
            pltpu.VMEM((2, 8, 16, 128), BF16),
            pltpu.VMEM(shape, BF16),
            pltpu.VMEM((C, 8, NZ), F32),
            pltpu.VMEM((1024, 1024), BF16),
            pltpu.VMEM((32, 128, 128), BF16),
            pltpu.VMEM((8, 4, C, 2 * C), BF16),
            pltpu.VMEM((2, 8, 16, 128), BF16),
            pltpu.VMEM((8, 16, 128), BF16),
            pltpu.VMEM((8, 16, 128), BF16),
            pltpu.VMEM((2, 64, 4, 128), BF16),
            pltpu.VMEM((2, 64, 4, 128), BF16),
            pltpu.VMEM((4, 64, 4, 128), BF16),
            pltpu.SemaphoreType.DMA((8,)),
            pltpu.SemaphoreType.DMA((9,)),
            pltpu.SemaphoreType.DMA,
            pltpu.SemaphoreType.DMA((4,)),
            pltpu.SemaphoreType.DMA((4,)),
            pltpu.SemaphoreType.DMA,
            pltpu.SemaphoreType.DMA((8, 2)),
            pltpu.SemaphoreType.DMA((2,)),
            pltpu.SemaphoreType.DMA((2,)),
        ],
        compiler_params=pltpu.CompilerParams(
            collective_id=0, has_side_effects=True, vmem_limit_bytes=32 << 20
        ),
    )(*(pltpu.with_memory_space_constraint(a, pltpu.HBM) for a in operands))
    grad_in, grad_spectral = pl.pallas_call(
        last_kernel,
        out_shape=(
            jax.ShapeDtypeStruct(shape, BF16),
            jax.ShapeDtypeStruct((4, C, 2 * C), F32),
        ),
        in_specs=[vmem] * 4,
        out_specs=(pl.BlockSpec(memory_space=pltpu.HBM),) * 2,
        scratch_shapes=[pltpu.VMEM(shape, BF16), pltpu.SemaphoreType.DMA((9,))],
        compiler_params=pltpu.CompilerParams(vmem_limit_bytes=24 << 20),
    )(*handed)
    return grad_in.reshape(activations.shape), grad_spectral


def solution(mesh):
    return jax.shard_map(
        body,
        mesh=mesh,
        in_specs=(
            P("dp", None, "space", None, None),
            P("dp", None, "space", None, None),
            P(("space", "dp"), None, None),
            P(),
            P(),
        ),
        out_specs=(P("dp", None, "space", None, None), P(("space", "dp"), None, None)),
        check_vma=False,
    )
```

```python
import jax
import jax.numpy as jnp
import numpy as np
from jax import lax
from jax.experimental import pallas as pl
from jax.experimental.pallas import tpu as pltpu
from jax.sharding import PartitionSpec as P

MX, MY, MZ = 16, 16, 8
NX, NY, NZ = 32, 48, 128
C = 64
GRP = 8
MESH = pl.DeviceIdType.MESH
F32, BF16 = jnp.float32, jnp.bfloat16


def centered(count):
    index = np.arange(count)
    return np.where(index < count // 2, index, index - count)


def tables():
    ty = 2 * np.pi * centered(MY)[:, None] * np.arange(NY)[None, :] / NY
    along_y = np.stack([np.cos(ty), -np.sin(ty)], 1)
    eye = np.eye(GRP)
    to_y = np.einsum("jry,cd->jrcdy", along_y, eye).reshape(MY * 2 * GRP, GRP * NY)
    tz = 2 * np.pi * np.arange(MZ)[:, None] * np.arange(NZ)[None, :] / NZ
    along_z = np.zeros((MZ, 2, 2, NZ))
    along_z[:, 0, 0], along_z[:, 0, 1] = np.cos(tz), np.sin(tz)
    along_z[:, 1, 0], along_z[:, 1, 1] = -np.sin(tz), np.cos(tz)
    weight = np.where(np.arange(MZ) == 0, 1.0, 2.0)[:, None, None, None]
    plain = along_z.reshape(MZ * 2, 2 * NZ)
    weighted = (along_z * weight).reshape(MZ * 2, 2 * NZ)
    s = 2 * np.pi * centered(MX)[None, :] * np.arange(NX)[:, None] / NX
    line = np.zeros((NX, 2, MX, 2))
    line[:, 0, :, 0], line[:, 0, :, 1] = np.cos(s), -np.sin(s)
    line[:, 1, :, 0], line[:, 1, :, 1] = np.sin(s), np.cos(s)
    line = line.reshape(NX // 2, 2, 2, MX, 2)
    to_q = np.einsum("shuqa,bd,ke->hakqbdseu", line, np.eye(4), np.eye(2)).reshape(512, 256)
    to_x = np.einsum("shuqa,bd,ke->hbskuaeqd", line, np.eye(4), np.eye(2)).reshape(512, 256)
    cast = lambda t: np.asarray(t.astype(np.float32)).astype(jnp.bfloat16)
    return tuple(cast(t) for t in (to_y, to_y.T.copy(), plain, weighted, to_q, to_x))


def dot(a, b, dims=((1,), (0,))):
    return lax.dot_general(a, b, (dims, ((), ())), preferred_element_type=F32)


def gelu_slope(value):
    density = lax.exp2(value * value * -0.7213475204444817)
    return 0.5 + (0.5 * lax.erf(value * 0.7071067811865476) + (value * 0.3989422804014327) * density)


def get_mid(mid, g):
    parts = []
    for x in range(2):
        rows = pl.ds(x * 64 + g * GRP, GRP)
        parts.append(mid[:, rows, :].reshape(2 * MY * GRP, NZ).astype(BF16))
    return jnp.concatenate(parts, axis=1)


def last_kernel(mid, loc, gsb, byt, out_h, gs_h, outb, sem):
    gs_out = pltpu.make_async_copy(gsb, gs_h, sem.at[8])
    gs_out.start()
    copies = []
    for g in range(8):
        rows = pl.ds(g * GRP, GRP)
        field = dot(byt[...], get_mid(mid, g))
        for x in range(2):
            value = field[:, x * NZ:(x + 1) * NZ].reshape(GRP, NY, NZ) + loc[rows, x]
            outb[rows, x] = value.astype(BF16)
        copies.append(pltpu.make_async_copy(outb.at[rows], out_h.at[rows], sem.at[g]))
        copies[g].start()
    for copy in copies + [gs_out]:
        copy.wait()


def kernel(
    act_h, cot_h, w_h, pw_h, off_h, by_h, byt_h, fz_h, fzw_h, bq_h, bx_h,
    mid, loc, gsb, byt,
    act, cot, w_own, pw_ref, off_ref, by, fz, fzw, bq, bx,
    mix, slope, offb, kron, wall, wbuf, spec, xin, din,
    send, back, land,
    in_sem, tab_sem, w_sem, ssem, rsem, wssem, wrsem, xssem, xrsem,
):
    dp = lax.axis_index("dp")
    s = lax.axis_index("space")
    zh, y = dp // 8, dp % 8
    me = zh * 16 + s
    low = lax.broadcasted_iota(jnp.int32, (1, 128), 1) < 64

    def far_first(k, half):
        return half + (1 - 2 * (k % 2)) * ((k + 1) // 2)

    z = 2 * zh + lax.rem(lax.div(s, 2), 2)
    zts = [lax.rem(z + k, 8) for k in range(8)]
    zhs = [lax.div(zt, 2) for zt in zts]
    xts = [lax.rem(lax.div(s, 4) + k, 4) * 4 for k in range(4)]
    slabs = [[xt + lax.rem(zt, 2) * 2 for xt in xts] for zt in zts]
    cores = [lax.rem(s, 2), lax.rem(s + 1, 2)]
    yys = [lax.rem(y + far_first(k, 4), 8) for k in range(8)]
    order = sorted(
        ((dz, dx, dc) for dz in range(8) for dx in range(4) for dc in range(2)),
        key=lambda d: (-min(d[0], 8 - d[0]) - min(d[1], 4 - d[1]), -d[2]),
    )

    def peer(n):
        dz, dx, dc = order[n]
        return zhs[dz], slabs[dz][dx] + cores[dc]

    def peer_y(n):
        return yys[n]

    bar = pltpu.get_barrier_semaphore()
    for n in range(63):
        zt, st = peer(n)
        pl.semaphore_signal(bar, inc=1, device_id=(zt * 8 + y, st), device_id_type=MESH)
    for n in range(7):
        pl.semaphore_signal(bar, inc=1, device_id=(zh * 8 + peer_y(n), s), device_id_type=MESH)

    def act_copy(g):
        rows = pl.ds(g * GRP, GRP)
        return pltpu.make_async_copy(act_h.at[rows], act.at[rows], in_sem.at[g])

    tabs = [
        pltpu.make_async_copy(h, v, tab_sem.at[i])
        for i, (h, v) in enumerate(
            ((by_h, by), (fz_h, fz), (bq_h, bq), (bx_h, bx), (byt_h, byt), (fzw_h, fzw), (pw_h, pw_ref), (off_h, off_ref), (cot_h, cot))
        )
    ]
    own_w = pltpu.make_async_copy(w_h, w_own, w_sem)
    tabs[0].start()
    for g in range(8):
        act_copy(g).start()
    own_w.start()
    for t in tabs[1:]:
        t.start()

    def lanes(ref, g):
        rows = pl.ds(g * GRP, GRP)
        return jnp.concatenate(
            [ref[rows, x].reshape(GRP * NY, NZ) for x in range(2)], axis=1
        )

    def put_mid(g, res):
        for x in range(2):
            rows = pl.ds(x * 64 + g * GRP, GRP)
            mid[:, rows, :] = res[:, x * NZ:(x + 1) * NZ].reshape(2 * MY, GRP, NZ)

    def forward_z(table, sbuf):
        for j in range(16):
            pair = jnp.concatenate([mid[2 * j].astype(BF16), mid[2 * j + 1].astype(BF16)], axis=1)
            res = dot(table[...], pair, ((1,), (1,)))
            sbuf[4 * j:4 * (j + 1)] = res.astype(BF16).reshape(4, 4, 128)

    def exchange(sbuf, st, to_owner):
        slot = me if to_owner else s * 4 + zh
        for n in range(64):
            zt, xt = peer(n)
            block = sbuf.at[xt * 4 + zt] if to_owner else sbuf.at[zt * 16 + xt]
            if n == 63:
                pltpu.make_async_copy(block, land.at[st, slot], rsem.at[st]).start()
            else:
                pltpu.make_async_remote_copy(
                    block, land.at[st, slot], ssem.at[st], rsem.at[st],
                    device_id=(zt * 8 + y, xt), device_id_type=MESH,
                ).start()

    def landed(st):
        whole = land.at[st]
        pltpu.make_async_copy(whole, whole, rsem.at[st]).wait()

    def share(src, dst, k):
        for n in range(7):
            yy = peer_y(n)
            pltpu.make_async_remote_copy(
                src.at[yy], dst.at[y], xssem.at[k], xrsem.at[k],
                device_id=(zh * 8 + yy, s), device_id_type=MESH,
            ).start()
        pltpu.make_async_copy(src.at[y], dst.at[y], xrsem.at[k]).start()

    def to_modes(st, scale):
        r = dot(bq[...], land[st].reshape(256, 128))
        first = jnp.where(low, r[0:128], r[384:512])
        second = jnp.where(low, r[128:256], r[256:384])
        return ((first + pltpu.roll(second, 64, 1)) * scale).astype(BF16)

    def from_modes(mixed, turned, scale):
        first = dot(bx[0:256], jnp.concatenate([mixed, turned], axis=0))
        second = dot(bx[256:512], jnp.concatenate([turned, mixed], axis=0))
        return (jnp.where(low, first, second) * scale).astype(BF16)

    def inverse_z(st, table):
        rows = land[st].reshape(256, 128)
        for j in range(16):
            res = dot(rows[16 * j:16 * (j + 1)], table[...], ((0,), (0,)))
            mid[2 * j] = res[:, :NZ]
            mid[2 * j + 1] = res[:, NZ:]

    which = (lax.broadcasted_iota(jnp.int32, (16, 1), 0) // 4)

    def kron_of(dims):
        rep = (
            lax.broadcasted_iota(jnp.int32, (1024, 64), 0) // 16
            == lax.broadcasted_iota(jnp.int32, (1024, 64), 1)
        ).astype(F32).astype(BF16)
        half = dot(rep, pw_ref[...], dims).astype(BF16)
        for m in range(4):
            full = dot(half[256 * m:256 * (m + 1)], rep, ((1,), (1,)))
            same = (
                lax.broadcasted_iota(jnp.int32, (256, 1024), 0) % 16
                == lax.broadcasted_iota(jnp.int32, (256, 1024), 1) % 16
            )
            kron[256 * m:256 * (m + 1), :] = jnp.where(same, full, 0.0).astype(BF16)

    def pointwise(src, with_offset, parts):
        def step(n, c):
            yb, m = n // 4, n % 4
            rows = pl.ds(pl.multiple_of(yb * 16, 16), 16)
            rhs = jnp.concatenate([src[:, x, rows, :].reshape(1024, NZ) for x in range(2)], axis=1)
            res = dot(kron[pl.ds(pl.multiple_of(m * 256, 256), 256), :], rhs)
            for x in range(2):
                part = res[:, x * NZ:(x + 1) * NZ].reshape(16, 2, 8, NZ)
                if with_offset:
                    part = part + offb[pl.ds(m * 16, 16)][:, None]
                loc[pl.ds(m * 16, 16), x, rows, :] = part.reshape(16, 16, NZ)
            return c

        lax.fori_loop(4 * parts[0], 4 * parts[1], step, 0)

    tabs[0].wait()

    def forward(g):
        act_copy(g).wait()
        put_mid(g, dot(by[...], lanes(act, g)))

    for g in range(8):
        forward(g)
    own_w.wait()
    tabs[1].wait()
    forward_z(fz, send.at[0])
    pl.semaphore_wait(bar, 70)

    def weights_to(src, owner, half, step):
        pltpu.make_async_remote_copy(
            src.at[pl.ds(2 * half, 2)], wbuf.at[owner, pl.ds(2 * half, 2)], wssem, wrsem.at[owner, half],
            device_id=(zh * 8 + (y + step) % 8, s), device_id_type=MESH,
        ).start()

    def weights_here(owner, half):
        here = wbuf.at[owner, pl.ds(2 * half, 2)]
        pltpu.make_async_copy(here, here, wrsem.at[owner, half]).wait()

    for step in (2, 1):
        for half in range(2):
            weights_to(w_own, y, half, step % 8)
            weights_to(w_own, y, 1 - half, -step % 8)
    exchange(send.at[0], 0, True)

    for t in tabs[2:]:
        t.wait()

    def spread(o, c):
        offb[o] = jnp.full((8, NZ), off_ref[o], F32)
        return c

    lax.fori_loop(0, C, spread, 0)
    kron_of(((1,), (1,)))

    before, behind = (y + 6) % 8, (y + 2) % 8
    for half in range(2):
        weights_here(before, half)
        weights_to(wbuf.at[before], before, half, 1)
        if half == 0:
            weights_to(wbuf.at[before], before, half, 2)
        weights_here(behind, 1 - half)
        weights_to(wbuf.at[behind], behind, 1 - half, 7)
        if half == 0:
            weights_to(wbuf.at[behind], behind, 1 - half, 6)

    pointwise(act, True, (0, 1))
    landed(0)
    spec[0] = to_modes(0, 1.0).reshape(8, 16, 128)
    share(spec.at[0], xin, 0)

    for n in range(8):
        yy = peer_y(7 - n)
        if n not in (0, 3, 4):
            weights_here(yy, 0)
            weights_here(yy, 1)
        w = (w_own if n == 0 else wbuf.at[yy])[...].reshape(4 * C, 2 * C)
        turned = pltpu.roll(w.astype(F32), 64, 1)
        rows = pl.ds(yy * 4, 4)
        wall[rows, 0:64, :] = w.reshape(4, C, 2 * C)
        wall[rows, 64:128, :] = jnp.where(low, -turned, turned).astype(BF16).reshape(4, C, 2 * C)
        x = spec[0, yy].astype(F32)
        x4 = jnp.concatenate([jnp.where(which == i, x, 0.0) for i in range(4)], axis=1).astype(BF16)
        res = dot(x4, wall[rows].reshape(512, 128))
        mix[0, yy] = res.astype(BF16)
        mix[1, yy] = pltpu.roll(res, 64, 1).astype(BF16)
    mixed = [mix[i].reshape(128, 128) for i in range(2)]
    back[0] = from_modes(*mixed, 1.0 / (NX * NY * NZ)).reshape(64, 4, 128)
    exchange(back.at[0], 1, False)
    pointwise(act, True, (1, 3))

    landed(1)
    inverse_z(1, fzw)

    def middle(g):
        rows = pl.ds(g * GRP, GRP)
        field = dot(byt[...], get_mid(mid, g))
        halves = []
        for x in range(2):
            value = field[:, x * NZ:(x + 1) * NZ].reshape(GRP, NY, NZ) + loc[rows, x]
            grad = (cot[rows, x].astype(F32) * gelu_slope(value)).astype(BF16)
            slope[rows, x] = grad
            halves.append(grad.reshape(GRP * NY, NZ))
        put_mid(g, dot(by[...], jnp.concatenate(halves, axis=1)))

    for g in range(8):
        middle(g)
    forward_z(fzw, send.at[1])
    exchange(send.at[1], 2, True)
    kron_of(((1,), (0,)))
    pointwise(slope, False, (0, 1))

    landed(2)
    spec_grad = to_modes(2, 1.0 / (NX * NY * NZ))
    spec[1] = spec_grad.reshape(8, 16, 128)
    mixed = []
    for t in range(8):
        res = dot(spec_grad[16 * t:16 * (t + 1)], wall[4 * t:4 * (t + 1)].reshape(512, 128), ((1,), (1,)))
        total = jnp.where(which == 0, res[:, 0:128], 0.0)
        for i in range(1, 4):
            total = total + jnp.where(which == i, res[:, 128 * i:128 * (i + 1)], 0.0)
        mixed.append(total)
    mixed = jnp.concatenate(mixed, axis=0)
    turned = pltpu.roll(mixed, 64, 1).astype(BF16)
    back[1] = from_modes(mixed.astype(BF16), turned, 1.0).reshape(64, 4, 128)
    exchange(back.at[1], 3, False)
    share(spec.at[1], din, 1)
    pointwise(slope, False, (1, 3))

    for k, buf in enumerate((xin, din)):
        pltpu.make_async_copy(buf, buf, xrsem.at[k]).wait()
    left = xin[...].reshape(128, 128).astype(F32)
    right = din[...].reshape(128, 128)
    mode = lax.broadcasted_iota(jnp.int32, (128, 1), 0) // 4 % 4
    for i in range(4):
        g = dot(jnp.where(mode == i, left, 0.0).astype(BF16), right, ((0,), (0,)))
        turned = pltpu.roll(g[64:128], 64, 1)
        gsb[i] = g[0:64] + jnp.where(low, turned, -turned)

    landed(3)
    inverse_z(3, fz)
    for st in range(4):
        sent = land.at[st, pl.ds(0, 63)]
        pltpu.make_async_copy(sent, sent, ssem.at[st]).wait()
    sent = wbuf.at[pl.ds(0, 7)]
    pltpu.make_async_copy(sent, sent, wssem).wait()
    for k in range(2):
        sent = xin.at[pl.ds(0, 7)]
        pltpu.make_async_copy(sent, sent, xssem.at[k]).wait()


def body(activations, cotangent, mode_weights, pointwise, offsets):
    shape = (C, 2, NY, NZ)
    consts = [jnp.asarray(t) for t in tables()]
    operands = (activations.reshape(shape), cotangent.reshape(shape), mode_weights, pointwise, offsets, *consts)
    hbm = pl.BlockSpec(memory_space=pltpu.HBM)
    vmem = pl.BlockSpec(memory_space=pltpu.VMEM)
    handed = pl.pallas_call(
        kernel,
        out_shape=(
            jax.ShapeDtypeStruct((2 * MY, 128, NZ), F32),
            jax.ShapeDtypeStruct(shape, F32),
            jax.ShapeDtypeStruct((4, C, 2 * C), F32),
            jax.ShapeDtypeStruct(consts[1].shape, BF16),
        ),
        in_specs=[hbm] * 11,
        out_specs=(vmem,) * 4,
        scratch_shapes=[
            pltpu.VMEM(shape, BF16),
            pltpu.VMEM(shape, BF16),
            pltpu.VMEM((4, C, 2 * C), BF16),
            pltpu.VMEM((C, C), BF16),
            pltpu.SMEM((C,), F32),
        ]
        + [pltpu.VMEM(t.shape, BF16) for t in consts[:1] + consts[2:]]
        + [
            pltpu.VMEM((2, 8, 16, 128), BF16),
            pltpu.VMEM(shape, BF16),
            pltpu.VMEM((C, 8, NZ), F32),
            pltpu.VMEM((1024, 1024), BF16),
            pltpu.VMEM((32, 128, 128), BF16),
            pltpu.VMEM((8, 4, C, 2 * C), BF16),
            pltpu.VMEM((2, 8, 16, 128), BF16),
            pltpu.VMEM((8, 16, 128), BF16),
            pltpu.VMEM((8, 16, 128), BF16),
            pltpu.VMEM((2, 64, 4, 128), BF16),
            pltpu.VMEM((2, 64, 4, 128), BF16),
            pltpu.VMEM((4, 64, 4, 128), BF16),
            pltpu.SemaphoreType.DMA((8,)),
            pltpu.SemaphoreType.DMA((9,)),
            pltpu.SemaphoreType.DMA,
            pltpu.SemaphoreType.DMA((4,)),
            pltpu.SemaphoreType.DMA((4,)),
            pltpu.SemaphoreType.DMA,
            pltpu.SemaphoreType.DMA((8, 2)),
            pltpu.SemaphoreType.DMA((2,)),
            pltpu.SemaphoreType.DMA((2,)),
        ],
        compiler_params=pltpu.CompilerParams(
            collective_id=0, has_side_effects=True, vmem_limit_bytes=32 << 20
        ),
    )(*(pltpu.with_memory_space_constraint(a, pltpu.HBM) for a in operands))
    grad_in, grad_spectral = pl.pallas_call(
        last_kernel,
        out_shape=(
            jax.ShapeDtypeStruct(shape, BF16),
            jax.ShapeDtypeStruct((4, C, 2 * C), F32),
        ),
        in_specs=[vmem] * 4,
        out_specs=(pl.BlockSpec(memory_space=pltpu.HBM),) * 2,
        scratch_shapes=[pltpu.VMEM(shape, BF16), pltpu.SemaphoreType.DMA((9,))],
        compiler_params=pltpu.CompilerParams(vmem_limit_bytes=24 << 20),
    )(*handed)
    return grad_in.reshape(activations.shape), grad_spectral


def solution(mesh):
    return jax.shard_map(
        body,
        mesh=mesh,
        in_specs=(
            P("dp", None, "space", None, None),
            P("dp", None, "space", None, None),
            P(("space", "dp"), None, None),
            P(),
            P(),
        ),
        out_specs=(P("dp", None, "space", None, None), P(("space", "dp"), None, None)),
        check_vma=False,
    )
```
